256 devices in a mesh: grp: 16 (over x, z_hi, core), mem: 16 (over z_lo, y).
Axes of the slice: x: 4, y: 4, z: 8 (z_hi: 2, z_lo: 4; z = z_hi * 4 + z_lo), core: 2. Of those that a mesh axis runs over, the one named last changes fastest.
Arguments:
- frames: bfloat16 [512, 256, 1024], P('grp', 'mem'), may hold values from -6 to 6
- probe_wave: float32 [2, 128, 128], P(None, 'mem'), may hold values from -6 to 6
Outputs:
- deconv_real: float32 [512, 256, 1024], P('mem', 'grp')
- deconv_imag: float32 [512, 256, 1024], P('mem', 'grp')
The draws below stay inside these ranges and needn't reach their ends.
All inputs are finite; a program needn't handle non-finite values.
Results may differ from the reference program's by a relative error of at most 0.0087.
Values may be sent and summed in bfloat16 or wider, within the bound.
A program may use at most 128 MiB of HBM per device.

```python
import math
import jax
import jax.numpy as jnp
from jax import lax

WIN = 32
SCAN_Y = 512
SCAN_X = 256
PIX = 1024
PROBE_N = 128
STRIDE_Y = 4
STRIDE_X = 2


def block_scale(key, shape, split, smallest, largest):
    factor_of = 1.0
    for dim, blocks in split:
        steps = jax.random.uniform(jax.random.fold_in(jax.random.fold_in(key, 6), dim), (blocks,), jnp.float32, smallest / len(split), largest / len(split))
        factor_of = factor_of * jnp.repeat(jnp.exp(steps), shape[dim] // blocks).reshape((-1,) + (1,) * (len(shape) - 1 - dim))
    return factor_of


def normal_values(own_key, extent, width, reach, split=(), kind=jnp.bfloat16):
    entries = width * jax.random.normal(own_key, extent, jnp.float32)
    if split:
        entries = entries * block_scale(own_key, extent, split, -0.22, 0.18)
    return jnp.clip(entries, -reach, reach).astype(kind)


def setup_inputs(seed: int = 0) -> dict:
    key_list = jax.random.split(jax.random.key(seed), 3)
    return {
        "frames": normal_values(key_list[0], (SCAN_Y, SCAN_X, PIX), 1.0, 6.0, ((0, 16), (1, 16))),
        "probe_wave": normal_values(key_list[1], (2, PROBE_N, PROBE_N), 1.0, 6.0, ((1, 16),), jnp.float32),
    }


wiener_floor = 0.5

def scan_table(length):
    positions = jnp.arange(length, dtype=jnp.int32)
    phases = positions[:, None] * positions[None, :] % length
    angles = -2.0 * math.pi / length * phases.astype(jnp.float32)
    factor = 1.0 / math.sqrt(length)
    return ((jnp.cos(angles) * factor).astype(jnp.bfloat16), (jnp.sin(angles) * factor).astype(jnp.bfloat16))

def detector_parts(window):
    offsets = jnp.arange(window, dtype=jnp.int32)
    phases = (offsets[:, None, None, None] * offsets[None, None, :, None] + offsets[None, :, None, None] * offsets[None, None, None, :]) % window
    phases = phases.reshape(window * window, window * window)
    angles = -2.0 * math.pi / window * phases.astype(jnp.float32)
    factor = 1.0 / window
    return ((jnp.cos(angles) * factor).astype(jnp.bfloat16), (jnp.sin(angles) * factor).astype(jnp.bfloat16))

def slab_table_of(part_re, part_im):
    upper = jnp.concatenate([part_re, part_im], axis=1)
    lower = jnp.concatenate([-part_im, part_re], axis=1)
    return jnp.concatenate([upper, lower], axis=0)

def signed_shift(freqs, length, step_size):
    centred = jnp.where(freqs >= length // 2, freqs - length, freqs)
    return jnp.floor_divide(centred, step_size).astype(jnp.int32)

def wigner_slab(probe_real, probe_imag, shift_y, shift_x, slab_table):
    grid_size = probe_real.shape[0]
    offsets = jnp.arange(WIN, dtype=jnp.int32)
    row_index = (offsets[None, :] + shift_y[:, None]) % grid_size
    col_index = (offsets[None, :] + shift_x[:, None]) % grid_size
    count_y = shift_y.shape[0]
    count_x = shift_x.shape[0]

    def shifted(plane):
        picked = jnp.take(plane, row_index, axis=0)
        picked = jnp.take(picked, col_index, axis=2)
        return picked.transpose(0, 2, 1, 3).reshape(count_y * count_x, WIN * WIN)
    moved_re = shifted(probe_real)
    moved_im = shifted(probe_imag)
    base_re = probe_real[:WIN, :WIN].reshape(1, WIN * WIN)
    base_im = probe_imag[:WIN, :WIN].reshape(1, WIN * WIN)
    prod_re = (base_re * moved_re + base_im * moved_im).astype(jnp.bfloat16)
    prod_im = (base_im * moved_re - base_re * moved_im).astype(jnp.bfloat16)
    stacked = jnp.concatenate([prod_re, prod_im], axis=1)
    slabs = jnp.dot(stacked, slab_table, preferred_element_type=jnp.float32)
    pixels = WIN * WIN
    slab_shape = (count_y, count_x, pixels)
    return (slabs[:, :pixels].reshape(slab_shape), slabs[:, pixels:].reshape(slab_shape))

def deconvolve(spec_re, spec_im, chi_re, chi_im):
    real_part = spec_re.astype(jnp.float32)
    imag_part = spec_im.astype(jnp.float32)
    denominator = chi_re * chi_re + chi_im * chi_im + wiener_floor
    out_re = (real_part * chi_re + imag_part * chi_im) / denominator
    out_im = (imag_part * chi_re - real_part * chi_im) / denominator
    return (out_re, out_im)

def swap_halves(values):
    half_width = values.shape[-1] // 2
    return jnp.concatenate([-values[..., half_width:], values[..., :half_width]], axis=-1)

def reference(frames, probe_wave):
    highest = lax.Precision.HIGHEST
    det_re, det_im = detector_parts(WIN)
    cy_re, cy_im = scan_table(SCAN_Y)
    cx_re, cx_im = scan_table(SCAN_X)
    cy_re32 = cy_re.astype(jnp.float32)
    cy_im32 = cy_im.astype(jnp.float32)
    cx_re32 = cx_re.astype(jnp.float32)
    cx_im32 = cx_im.astype(jnp.float32)
    flat_rows = frames.reshape(SCAN_Y * SCAN_X, PIX)
    column_groups = 8
    group_width = PIX // column_groups
    re_cols = det_re.reshape(PIX, column_groups, group_width).transpose(1, 0, 2)
    im_cols = det_im.reshape(PIX, column_groups, group_width).transpose(1, 0, 2)

    def one_block(columns):
        cols_re, cols_im = columns
        merged = jnp.concatenate([cols_re, cols_im], axis=1)
        spatial = jnp.dot(flat_rows, merged, preferred_element_type=jnp.float32).astype(jnp.bfloat16)
        spatial = lax.optimization_barrier(spatial)
        spatial = spatial.reshape(SCAN_Y, SCAN_X, 2 * group_width).astype(jnp.float32)
        along_x = jnp.einsum('yrc,rq->yqc', spatial, cx_re32, precision=highest)
        along_x = along_x + jnp.einsum('yrc,rq->yqc', swap_halves(spatial), cx_im32, precision=highest)
        both = jnp.einsum('rxc,rq->qxc', along_x, cy_re32, precision=highest)
        both = both + jnp.einsum('rxc,rq->qxc', swap_halves(along_x), cy_im32, precision=highest)
        return both.astype(jnp.bfloat16)
    spectra = lax.map(one_block, (re_cols, im_cols))
    spectra = spectra.reshape(column_groups, SCAN_Y, SCAN_X, 2, group_width)
    spec_re = spectra[:, :, :, 0, :].transpose(1, 2, 0, 3).reshape(SCAN_Y, SCAN_X, PIX)
    spec_im = spectra[:, :, :, 1, :].transpose(1, 2, 0, 3).reshape(SCAN_Y, SCAN_X, PIX)
    spec_re = lax.optimization_barrier(spec_re)
    spec_im = lax.optimization_barrier(spec_im)
    spec_re = spec_re.reshape(PROBE_N, STRIDE_Y, SCAN_X, PIX)
    spec_im = spec_im.reshape(PROBE_N, STRIDE_Y, SCAN_X, PIX)
    slab_table = slab_table_of(det_re, det_im)
    shift_x = signed_shift(jnp.arange(PROBE_N, dtype=jnp.int32) * STRIDE_X, SCAN_X, STRIDE_X)
    group_ids = jnp.arange(PROBE_N, dtype=jnp.int32)

    def one_group(inputs):
        group_index, rows_re, rows_im = inputs
        shift_y = signed_shift(group_index[None] * STRIDE_Y, SCAN_Y, STRIDE_Y)
        chi_re, chi_im = wigner_slab(probe_wave[0], probe_wave[1], shift_y, shift_x, slab_table)
        chi_re = jnp.repeat(chi_re, STRIDE_X, axis=1)
        chi_im = jnp.repeat(chi_im, STRIDE_X, axis=1)
        return deconvolve(rows_re, rows_im, chi_re, chi_im)
    out_re, out_im = lax.map(one_group, (group_ids, spec_re, spec_im))
    return (out_re.reshape(SCAN_Y, SCAN_X, PIX), out_im.reshape(SCAN_Y, SCAN_X, PIX))
```

```python
import functools
import math

import jax
import jax.numpy as jnp
import ml_dtypes
import numpy as np
from jax import lax
from jax.experimental import pallas as pl
from jax.experimental.pallas import tpu as pltpu
from jax.sharding import PartitionSpec as P

WIN = 32
SCAN_Y = 512
SCAN_X = 256
PIX = 1024
MESH = pl.DeviceIdType.MESH
F32 = jnp.float32
BF16 = jnp.bfloat16

wiener_floor = 0.5


def scan_table(length):
    positions = np.arange(length)
    phases = (positions[:, None] * positions[None, :]) % length
    angles = -2.0 * math.pi / length * phases
    factor = 1.0 / math.sqrt(length)
    real = (np.cos(angles) * factor).astype(np.float32).astype(ml_dtypes.bfloat16)
    imag = (np.sin(angles) * factor).astype(np.float32).astype(ml_dtypes.bfloat16)
    return real, imag


def tables():
    yr, yi = scan_table(SCAN_Y)
    wy = np.concatenate([yr, yi], axis=1)
    xr, xi = scan_table(SCAN_X)
    wx = np.stack([np.concatenate([xr, -xi], axis=1), np.concatenate([xi, xr], axis=1)])
    perm = np.zeros((512, 512), ml_dtypes.bfloat16)
    src = np.arange(512)
    perm[src, (src // 32 % 4) * 128 + (src // 128) * 32 + src % 32] = 1
    pos = np.arange(WIN)
    angle = 2.0 * math.pi / WIN * (pos[:, None] * pos[None, :] % WIN)
    cos, sin = np.cos(angle), np.sin(angle)
    det = np.stack(
        [np.repeat(cos, WIN, 1), np.repeat(sin, WIN, 1), np.tile(cos, (1, WIN)) / WIN, np.tile(sin, (1, WIN)) / WIN]
    ).astype(np.float32)
    return wy, wx, perm, det


def dot(a, b):
    return jnp.dot(a, b, preferred_element_type=F32)


def arrange_frames(x, xs, ms, m1):
    for lt in range(8):
        xs[lt] = x[:, lt * 128 : (lt + 1) * 128].astype(F32)

    @pl.loop(0, 16)
    def _(xl):
        for dh in range(2):
            block = jnp.concatenate([xs[kk * 2 + dh, pl.ds(xl, 32, stride=16), :] for kk in range(4)], axis=0)
            ms[pl.ds(dh * 2048 + xl, 128, stride=16), :] = block.T

    m1[...] = ms[...].astype(BF16)


def detector_table(det, ddr, ddi):
    @pl.loop(0, 32)
    def _(ky):
        ca, sa = det[0, pl.ds(ky, 1), :], det[1, pl.ds(ky, 1), :]
        cb, sb = det[2], det[3]
        real = cb * ca - sb * sa
        imag = -(sb * ca + cb * sa)
        h = ky // 16
        upper = pl.multiple_of((ky % 16) * 32, 32)
        lower = pl.multiple_of(upper + 512, 32)
        ddr[h, pl.ds(upper, 32), :] = real.astype(BF16)
        ddr[h, pl.ds(lower, 32), :] = (-imag).astype(BF16)
        ddi[h, pl.ds(upper, 32), :] = imag.astype(BF16)
        ddi[h, pl.ds(lower, 32), :] = real.astype(BF16)


def probe_products(g, m, prb, pf):
    lane = lax.broadcasted_iota(jnp.int32, (8, 128), 1)
    row = lax.broadcasted_iota(jnp.int32, (8, 128), 0)
    group = lane // 32

    def flat(x, j):
        w = pltpu.roll(x, (128 - j) % 128, 1) if j else x
        y = w
        for q in range(1, 4):
            y = jnp.where(group == q, pltpu.roll(w, 32 * q, 1), y)
        return [jnp.sum(jnp.where(row == group + 4 * half, y, 0.0), axis=0, keepdims=True) for half in range(2)]

    base = []
    ext = []
    for c in range(2):
        tiles = []
        for q in range(4):
            tiles += flat(prb[q, c], 0)
        base.append([jnp.broadcast_to(t, (8, 128)) for t in tiles])
        tiles = []
        for q in range(5):
            x = pltpu.roll(prb[lax.rem(m + q, 16), c], lax.rem(128 - 8 * g, 128), 1)
            halves = [jnp.zeros((8, 128), F32)] * 2
            for j in range(8):
                sums = flat(x, j)
                halves = [jnp.where(row == j, jnp.broadcast_to(s, (8, 128)), h) for s, h in zip(sums, halves)]
            tiles += halves
        ext.append(tiles)
    for i in range(8):
        off, turn = i // 4, i % 4
        moved = []
        for c in range(2):
            if turn:
                rolled = [pltpu.roll(t, 128 - 32 * turn, 1) for t in ext[c]]
                moved.append([jnp.where(group < 4 - turn, rolled[t + off], rolled[t + off + 1]) for t in range(8)])
            else:
                moved.append([ext[c][t + off] for t in range(8)])
        for t in range(8):
            br, bi, mr, mi = base[0][t], base[1][t], moved[0][t], moved[1][t]
            h, at = t // 4, (t % 4) * 128
            pf[h, i * 8 : i * 8 + 8, at : at + 128] = br * mr + bi * mi
            pf[h, i * 8 : i * 8 + 8, 512 + at : 512 + at + 128] = bi * mr - br * mi


def wiener_gain(pf, ddr, ddi, gr, gi, ger, gei):
    left, right = pf[0].astype(BF16), pf[1].astype(BF16)
    chi_re = dot(left, ddr[0]) + dot(right, ddr[1])
    chi_im = dot(left, ddi[0]) + dot(right, ddi[1])
    scale = 1.0 / (chi_re * chi_re + chi_im * chi_im + wiener_floor)
    gr[...] = chi_re * scale
    gi[...] = chi_im * scale
    row = lax.broadcasted_iota(jnp.int32, (8, 1024), 0)

    @pl.loop(0, 8)
    def _(j):
        for src, dst in ((gr, ger), (gi, gei)):
            for t in range(4):
                first = jnp.broadcast_to(src[pl.ds(16 * t + j, 1), :], (8, 1024))
                second = jnp.broadcast_to(src[pl.ds(16 * t + 8 + j, 1), :], (8, 1024))
                dst[j, t * 8 : t * 8 + 8, :] = jnp.where(row < 4, first, second)


def scan_transform(h, r, rp, cst, f, m2, wy, wx, perm):
    if h == 0:

        @pl.loop(0, 4)
        def _(j):
            lhs = jnp.concatenate([r[pl.ds(pl.multiple_of((4 * j + t) * 256, 256), 256), :] for t in range(4)], axis=1)
            moved = dot(lhs, perm[...]).astype(BF16)
            for kk in range(4):
                rp[kk, j] = moved[:, kk * 128 : (kk + 1) * 128]

    @pl.loop(0, 2)
    def _(k2):
        kk = 2 * h + k2
        lhs = jnp.concatenate([rp[kk, j] for j in range(4)], axis=1)
        for c in range(2):
            cst[c * 256 : (c + 1) * 256, :] = dot(lhs, wy[:, c * 512 : (c + 1) * 512]).astype(BF16)
        for c in range(2):
            res = dot(wx[c], cst[...]).astype(BF16)
            for t in range(4):
                f[t, 2 * c + k2] = res[:, t * 128 : (t + 1) * 128]

    @pl.loop(0, 4)
    def _(t):
        lhs = jnp.concatenate([f[t, s] for s in range(4)], axis=1)
        res = dot(lhs, perm[...]).astype(BF16)
        for q in range(4):
            m2[h, 4 * t + q] = res[:, q * 128 : (q + 1) * 128]


def gather_pixels(h, r2, z, low):
    z[...] = r2[h].astype(F32)

    @pl.loop(0, 16)
    def _(v):
        halves = [z[pl.ds(dh * 2048 + v, 128, stride=16), :].T for dh in range(2)]
        turned = jnp.concatenate(halves, axis=1).astype(BF16)
        rows = jnp.concatenate([turned[s * 32 : (s + 1) * 32, :] for s in range(4)], axis=1)
        low[h, pl.ds(pl.multiple_of(v * 32, 32), 32), :] = rows


def kernel(
    frames, probe, wy_h, wx_h, perm_h, det_h, out_re, out_im,
    x, pv, prb, wy, wx, perm, det, xs, m1, r, rp, cst, f, m2, r2, low, ddr, ddi, pf, gr, gi, ger, gei, sre, sim, o,
    load_sem, prb_send, prb_recv, send, recv, out_sem,
):
    g, m = lax.axis_index("grp"), lax.axis_index("mem")
    me = g * 16 + m

    def peer(i):
        return lax.rem(g + i // 16, 16), lax.rem(m + lax.rem(i, 16), 16)

    loads = [
        pltpu.make_async_copy(src, dst, load_sem.at[n])
        for n, (src, dst) in enumerate(
            ((frames, x), (probe, pv), (wy_h, wy), (wx_h, wx), (perm_h, perm), (det_h, det))
        )
    ]
    for load in loads:
        load.start()
    barrier = pltpu.get_barrier_semaphore()

    @pl.loop(1, 256)
    def _(i):
        pl.semaphore_signal(barrier, inc=1, device_id=peer(i), device_id_type=MESH)

    loads[0].wait()
    loads[1].wait()
    arrange_frames(x, xs, o.at[0], m1)
    pl.semaphore_wait(barrier, 255)

    pltpu.make_async_copy(pv, prb.at[m], prb_recv).start()

    @pl.loop(1, 16)
    def _(i):
        pltpu.make_async_remote_copy(
            src_ref=pv, dst_ref=prb.at[m], send_sem=prb_send, recv_sem=prb_recv,
            device_id=(g, lax.rem(m + i, 16)), device_id_type=MESH,
        ).start()

    here = pl.ds(pl.multiple_of(me * 16, 16), 16)
    pltpu.make_async_copy(m1.at[here], r.at[here], recv.at[0]).start()

    @pl.loop(1, 256)
    def _(i):
        a, b = peer(i)
        there = pl.ds(pl.multiple_of((a * 16 + b) * 16, 16), 16)
        pltpu.make_async_remote_copy(
            src_ref=m1.at[there], dst_ref=r.at[here], send_sem=send.at[0], recv_sem=recv.at[0],
            device_id=(a, b), device_id_type=MESH,
        ).start()

    for load in loads[2:]:
        load.wait()
    detector_table(det, ddr, ddi)
    pltpu.make_async_copy(prb, prb, prb_recv).wait()
    probe_products(g, m, prb, pf)
    pltpu.make_async_copy(r, r, recv.at[0]).wait()

    for h in range(2):
        scan_transform(h, r, rp, cst, f, m2, wy, wx, perm)
        own = pl.ds(pl.multiple_of(g * 16, 16), 16)
        pltpu.make_async_copy(m2.at[h, m, own], r2.at[h, here], recv.at[1 + h]).start()

        @pl.loop(1, 256)
        def _(i):
            a, b = peer(i)
            there = pl.ds(pl.multiple_of(a * 16, 16), 16)
            pltpu.make_async_remote_copy(
                src_ref=m2.at[h, b, there], dst_ref=r2.at[h, here], send_sem=send.at[1 + h], recv_sem=recv.at[1 + h],
                device_id=(a, b), device_id_type=MESH,
            ).start()

    wiener_gain(pf, ddr, ddi, gr, gi, ger, gei)

    pltpu.make_async_copy(r2.at[0], r2.at[0], recv.at[1]).wait()
    gather_pixels(0, r2, o.at[0], low)

    @pl.loop(0, 4)
    def _(n):
        lanes = pl.ds(pl.multiple_of(n * 256, 256), 256)
        sre[n] = dot(low[0], ddr[0, :, lanes])
        sim[n] = dot(low[0], ddi[0, :, lanes])

    pltpu.make_async_copy(r2.at[1], r2.at[1], recv.at[2]).wait()
    gather_pixels(1, r2, o.at[0], low)
    oo = o

    @pl.loop(0, 4)
    def _(n):
        lanes = pl.ds(pl.multiple_of(n * 256, 256), 256)
        sre[n] += dot(low[1], ddr[1, :, lanes])
        sim[n] += dot(low[1], ddi[1, :, lanes])

        for lt in range(2):
            part = pl.ds(pl.multiple_of(n * 256 + lt * 128, 128), 128)

            @pl.loop(0, 16)
            def _(v):
                rows = pl.ds(pl.multiple_of(v * 32, 32), 32)
                s_re, s_im = sre[n, rows, lt * 128 : (lt + 1) * 128], sim[n, rows, lt * 128 : (lt + 1) * 128]
                g_re, g_im = ger[v // 2, :, part], gei[v // 2, :, part]
                spot = pl.ds((2 * n + lt) * 512 + v, 32, stride=16)
                oo[0, spot, :] = s_re * g_re + s_im * g_im
                oo[1, spot, :] = s_im * g_re - s_re * g_im

            block = pl.ds(pl.multiple_of((2 * n + lt) * 512, 512), 512)
            pltpu.make_async_copy(oo.at[0, block], out_re.at[:, part], out_sem.at[0]).start()
            pltpu.make_async_copy(oo.at[1, block], out_im.at[:, part], out_sem.at[1]).start()

    pltpu.make_async_copy(prb.at[pl.ds(0, 15)], prb.at[pl.ds(0, 15)], prb_send).wait()
    for n in range(3):
        sent = pl.ds(0, 255 * 16)
        pltpu.make_async_copy(r.at[sent], r.at[sent], send.at[n]).wait()
    pltpu.make_async_copy(oo.at[0], out_re, out_sem.at[0]).wait()
    pltpu.make_async_copy(oo.at[1], out_im, out_sem.at[1]).wait()


def fused(frames, probe):
    wy, wx, perm, det = (jnp.asarray(t) for t in tables())
    hbm = pl.BlockSpec(memory_space=pl.ANY)
    dma = pltpu.SemaphoreType.DMA
    return pl.pallas_call(
        kernel,
        out_shape=(jax.ShapeDtypeStruct((512, 1024), F32),) * 2,
        in_specs=[hbm] * 6,
        out_specs=(hbm, hbm),
        scratch_shapes=[
            pltpu.VMEM((512, 1024), BF16),
            pltpu.VMEM((2, 8, 128), F32),
            pltpu.VMEM((16, 2, 8, 128), F32),
            pltpu.VMEM((512, 1024), BF16),
            pltpu.VMEM((2, 256, 512), BF16),
            pltpu.VMEM((512, 512), BF16),
            pltpu.VMEM((4, 32, 1024), F32),
            pltpu.VMEM((8, 512, 128), F32),
            pltpu.VMEM((4096, 128), BF16),
            pltpu.VMEM((4096, 128), BF16),
            pltpu.VMEM((4, 4, 256, 128), BF16),
            pltpu.VMEM((512, 512), BF16),
            pltpu.VMEM((4, 4, 256, 128), BF16),
            pltpu.VMEM((2, 16, 256, 128), BF16),
            pltpu.VMEM((2, 4096, 128), BF16),
            pltpu.VMEM((2, 512, 1024), BF16),
            pltpu.VMEM((2, 1024, 1024), BF16),
            pltpu.VMEM((2, 1024, 1024), BF16),
            pltpu.VMEM((2, 64, 1024), F32),
            pltpu.VMEM((64, 1024), F32),
            pltpu.VMEM((64, 1024), F32),
            pltpu.VMEM((8, 32, 1024), F32),
            pltpu.VMEM((8, 32, 1024), F32),
            pltpu.VMEM((4, 512, 256), F32),
            pltpu.VMEM((4, 512, 256), F32),
            pltpu.VMEM((2, 4096, 128), F32),
            dma((6,)), dma, dma, dma((3,)), dma((3,)), dma((2,)),
        ],
        compiler_params=pltpu.CompilerParams(collective_id=0, has_side_effects=True, vmem_limit_bytes=60 << 20),
    )(frames, probe, wy, wx, perm, det)


def shards(frames, probe_wave):
    real, imag = fused(frames.reshape(512, PIX), probe_wave)
    return real.reshape(32, 16, PIX), imag.reshape(32, 16, PIX)


def solution(mesh):
    return jax.shard_map(
        shards,
        mesh=mesh,
        in_specs=(P("grp", "mem", None), P(None, "mem", None)),
        out_specs=(P("mem", "grp", None), P("mem", "grp", None)),
        check_vma=False,
    )
```

```python
import math

import jax
import jax.numpy as jnp
import ml_dtypes
import numpy as np
from jax import lax
from jax.experimental import pallas as pl
from jax.experimental.pallas import tpu as pltpu
from jax.sharding import PartitionSpec as P

WIN = 32
SCAN_Y = 512
SCAN_X = 256
PIX = 1024
MESH = pl.DeviceIdType.MESH
F32 = jnp.float32
BF16 = jnp.bfloat16

wiener_floor = 0.5


def scan_table(length):
    positions = np.arange(length)
    phases = (positions[:, None] * positions[None, :]) % length
    angles = -2.0 * math.pi / length * phases
    factor = 1.0 / math.sqrt(length)
    real = (np.cos(angles) * factor).astype(np.float32).astype(ml_dtypes.bfloat16)
    imag = (np.sin(angles) * factor).astype(np.float32).astype(ml_dtypes.bfloat16)
    return real, imag


def tables():
    yr, yi = scan_table(SCAN_Y)
    wy = np.concatenate([yr, yi], axis=1)
    xr, xi = scan_table(SCAN_X)
    order = np.arange(SCAN_X).reshape(16, 8, 2).transpose(2, 0, 1).reshape(-1)
    xr, xi = xr[:, order], xi[:, order]
    wx = np.stack([np.concatenate([xr, -xi], axis=1), np.concatenate([xi, xr], axis=1)])
    perm = np.zeros((512, 512), ml_dtypes.bfloat16)
    src = np.arange(512)
    perm[src, (src // 32 % 4) * 128 + (src // 128) * 32 + src % 32] = 1
    pos = np.arange(WIN)
    angle = 2.0 * math.pi / WIN * (pos[:, None] * pos[None, :] % WIN)
    cos, sin = np.cos(angle), np.sin(angle)
    det = np.stack(
        [np.repeat(cos, WIN, 1), np.repeat(sin, WIN, 1), np.tile(cos, (1, WIN)) / WIN, np.tile(sin, (1, WIN)) / WIN]
    ).astype(np.float32)
    return wy, wx, perm, det


def dot(a, b):
    return jnp.dot(a, b, preferred_element_type=F32)


def arrange_frames(h, x, xs, ms, m1):
    for lt in range(4):
        xs[lt] = x[:, h * 512 + lt * 128 : h * 512 + (lt + 1) * 128].astype(F32)

    @pl.loop(0, 8)
    def _(x8):
        for dh in range(2):
            block = jnp.concatenate(
                [xs[k2 * 2 + dh, pl.ds(2 * x8 + x2, 32, stride=16), :] for k2 in range(2) for x2 in range(2)], axis=0
            )
            ms[pl.ds(dh * 1024 + x8, 128, stride=8), :] = block.T

    m1[h] = ms[0:2048, :].reshape(256, 8, 128).astype(BF16)


def detector_table(det, ddr, ddi):
    @pl.loop(0, 32)
    def _(ky):
        ca, sa = det[0, pl.ds(ky, 1), :], det[1, pl.ds(ky, 1), :]
        cb, sb = det[2], det[3]
        real = cb * ca - sb * sa
        imag = -(sb * ca + cb * sa)
        h = ky // 16
        upper = pl.multiple_of((ky % 16) * 32, 32)
        lower = pl.multiple_of(upper + 512, 32)
        ddr[h, pl.ds(upper, 32), :] = real.astype(BF16)
        ddr[h, pl.ds(lower, 32), :] = (-imag).astype(BF16)
        ddi[h, pl.ds(upper, 32), :] = imag.astype(BF16)
        ddi[h, pl.ds(lower, 32), :] = real.astype(BF16)


def probe_products(g, m, prb, pf):
    lane = lax.broadcasted_iota(jnp.int32, (8, 128), 1)
    row = lax.broadcasted_iota(jnp.int32, (8, 128), 0)
    group = lane // 32

    def flat(x, j):
        w = pltpu.roll(x, (128 - j) % 128, 1) if j else x
        y = w
        for q in range(1, 4):
            y = jnp.where(group == q, pltpu.roll(w, 32 * q, 1), y)
        return [jnp.sum(jnp.where(row == group + 4 * half, y, 0.0), axis=0, keepdims=True) for half in range(2)]

    base = []
    ext = []
    for c in range(2):
        tiles = []
        for q in range(4):
            tiles += flat(prb[q, c], 0)
        base.append([jnp.broadcast_to(t, (8, 128)) for t in tiles])
        tiles = []
        for q in range(5):
            x = pltpu.roll(prb[lax.rem(m + q, 16), c], lax.rem(128 - 8 * g, 128), 1)
            halves = [jnp.zeros((8, 128), F32)] * 2
            for j in range(8):
                sums = flat(x, j)
                halves = [jnp.where(row == j, jnp.broadcast_to(s, (8, 128)), h) for s, h in zip(sums, halves)]
            tiles += halves
        ext.append(tiles)
    for i in range(8):
        off, turn = i // 4, i % 4
        moved = []
        for c in range(2):
            if turn:
                rolled = [pltpu.roll(t, 128 - 32 * turn, 1) for t in ext[c]]
                moved.append([jnp.where(group < 4 - turn, rolled[t + off], rolled[t + off + 1]) for t in range(8)])
            else:
                moved.append([ext[c][t + off] for t in range(8)])
        for t in range(8):
            br, bi, mr, mi = base[0][t], base[1][t], moved[0][t], moved[1][t]
            h, at = t // 4, (t % 4) * 128
            pf[h, i * 8 : i * 8 + 8, at : at + 128] = br * mr + bi * mi
            pf[h, i * 8 : i * 8 + 8, 512 + at : 512 + at + 128] = bi * mr - br * mi


def wiener_gain(pf, ddr, ddi, gain):
    left, right = pf[0].astype(BF16), pf[1].astype(BF16)
    chi_re = dot(left, ddr[0]) + dot(right, ddr[1])
    chi_im = dot(left, ddi[0]) + dot(right, ddi[1])
    scale = 1.0 / (chi_re * chi_re + chi_im * chi_im + wiener_floor)
    gain[0] = chi_re * scale
    gain[1] = chi_im * scale


def scan_transform(h, r, rp, cst, f, store, wy, wx, perm):
    @pl.loop(0, 4)
    def _(j):
        parts = [r[h, pl.ds((4 * j + t) * 16, 16)].astype(F32).reshape(128, 128) for t in range(4)]
        moved = dot(jnp.concatenate(parts, axis=1).astype(BF16), perm[...]).astype(BF16)
        for s in range(4):
            rp[s, j] = moved[:, s * 128 : (s + 1) * 128]

    @pl.loop(0, 2)
    def _(k2):
        lhs = jnp.concatenate(
            [jnp.concatenate([rp[2 * k2 + x2, j] for j in range(4)], axis=1) for x2 in range(2)], axis=0
        )
        for c in range(2):
            cst[c * 256 : (c + 1) * 256, :] = dot(lhs, wy[:, c * 512 : (c + 1) * 512]).astype(BF16)
        for c in range(2):
            res = dot(wx[c], cst[...]).astype(BF16)
            for t in range(4):
                f[t, 2 * c + k2] = res[:, t * 128 : (t + 1) * 128]

    @pl.loop(0, 4)
    def _(t):
        lhs = jnp.concatenate([f[t, s] for s in range(4)], axis=1)
        res = dot(lhs, perm[...])
        for q in range(4):
            store(4 * t + q, res[:, q * 128 : (q + 1) * 128])


def gather_pixels(z, count, low, first):
    @pl.loop(0, count)
    def _(v):
        halves = [z[pl.ds(dh * 128 * count + v, 128, stride=count), :].T for dh in range(2)]
        turned = jnp.concatenate(halves, axis=1).astype(BF16)
        rows = jnp.concatenate([turned[s * 32 : (s + 1) * 32, :] for s in range(4)], axis=1)
        low[pl.ds(pl.multiple_of(first + v * 32, 32), 32), :] = rows


def exchange_kernel(
    frames, probe, wy_h, wx_h, perm_h, det_h, spec_out, gain_out,
    x, pv, prb, wy, wx, perm, det, xs, z, m1, r, rp, cst, f, m2, m3, r2, r3, low, ddr, ddi, pf, gain, sre, sim, spec,
    load_sem, prb_send, prb_recv, send, recv, out_sem,
):
    g, m = lax.axis_index("grp"), lax.axis_index("mem")
    me = g * 16 + m

    def to_all(act):
        @pl.loop(1, 16)
        def _(i):
            act(g, lax.rem(m + i, 16))

        @pl.loop(1, 16)
        def _(i):
            a = lax.rem(g + i, 16)

            @pl.loop(0, 16)
            def _(j):
                act(a, lax.rem(m + j, 16))

    def push(n, src, dst, a, b):
        pltpu.make_async_remote_copy(
            src_ref=src, dst_ref=dst, send_sem=send.at[n], recv_sem=recv.at[n], device_id=(a, b), device_id_type=MESH
        ).start()

    def arrived(n, ref):
        pltpu.make_async_copy(ref, ref, recv.at[n]).wait()

    loads = [
        pltpu.make_async_copy(src, dst, load_sem.at[n])
        for n, (src, dst) in enumerate(
            ((frames, x), (probe, pv), (wy_h, wy), (wx_h, wx), (perm_h, perm), (det_h, det))
        )
    ]
    for load in loads:
        load.start()
    barrier = pltpu.get_barrier_semaphore()
    to_all(lambda a, b: pl.semaphore_signal(barrier, inc=1, device_id=(a, b), device_id_type=MESH))

    loads[0].wait()
    loads[1].wait()
    for h in range(2):
        arrange_frames(h, x, xs, z, m1)
    pl.semaphore_wait(barrier, 255)

    for h in range(2):
        pltpu.make_async_copy(m1.at[h, me], r.at[h, me], recv.at[h]).start()
        to_all(lambda a, b: push(h, m1.at[h, a * 16 + b], r.at[h, me], a, b))
        if h == 0:
            pltpu.make_async_copy(pv, prb.at[m], prb_recv).start()

            @pl.loop(1, 16)
            def _(i):
                pltpu.make_async_remote_copy(
                    src_ref=pv, dst_ref=prb.at[m], send_sem=prb_send, recv_sem=prb_recv,
                    device_id=(g, lax.rem(m + i, 16)), device_id_type=MESH,
                ).start()

    for load in loads[2:]:
        load.wait()

    arrived(0, r.at[0])

    def store_first(b, tile):
        m2[b] = tile.astype(BF16)

    scan_transform(0, r, rp, cst, f, store_first, wy, wx, perm)
    here = pl.ds(pl.multiple_of(me * 16, 16), 16)
    pltpu.make_async_copy(m2.at[m, pl.ds(pl.multiple_of(g * 16, 16), 16)], r2.at[here], recv.at[2]).start()
    to_all(lambda a, b: push(2, m2.at[b, pl.ds(pl.multiple_of(a * 16, 16), 16)], r2.at[here], a, b))

    arrived(1, r.at[1])

    def store_second(b, tile):
        m3[b] = tile.reshape(32, 8, 128).astype(BF16)

    scan_transform(1, r, rp, cst, f, store_second, wy, wx, perm)
    for half in range(2):
        pltpu.make_async_copy(m3.at[m, 2 * g + half], r3.at[half, me], recv.at[3 + half]).start()
        to_all(lambda a, b: push(3 + half, m3.at[b, 2 * a + half], r3.at[half, me], a, b))

    detector_table(det, ddr, ddi)
    pltpu.make_async_copy(prb, prb, prb_recv).wait()
    probe_products(g, m, prb, pf)
    wiener_gain(pf, ddr, ddi, gain)
    gain_copy = pltpu.make_async_copy(gain, gain_out, out_sem.at[0])
    gain_copy.start()

    arrived(2, r2)
    z[...] = r2[...].astype(F32)
    gather_pixels(z, 16, low, 0)

    @pl.loop(0, 4)
    def _(n):
        lanes = pl.ds(pl.multiple_of(n * 256, 256), 256)
        sre[n] = dot(low[...], ddr[0, :, lanes])
        sim[n] = dot(low[...], ddi[0, :, lanes])

    copies = []
    for half in range(2):
        arrived(3 + half, r3.at[half])
        z[0:2048, :] = r3[half].astype(F32).reshape(2048, 128)
        gather_pixels(z, 8, low, half * 256)
        rows = slice(half * 256, (half + 1) * 256)

        @pl.loop(0, 4)
        def _(n):
            lanes = pl.ds(pl.multiple_of(n * 256, 256), 256)
            spec[0, rows, lanes] = (sre[n, rows, :] + dot(low[rows, :], ddr[1, :, lanes])).astype(BF16)
            spec[1, rows, lanes] = (sim[n, rows, :] + dot(low[rows, :], ddi[1, :, lanes])).astype(BF16)

        copies.append(pltpu.make_async_copy(spec.at[:, rows], spec_out.at[:, rows], out_sem.at[1 + half]))
        copies[-1].start()

    pltpu.make_async_copy(prb.at[pl.ds(0, 15)], prb.at[pl.ds(0, 15)], prb_send).wait()
    for n, ref in enumerate((r.at[0], r.at[1], None, r3.at[0], r3.at[1])):
        ref = r2.at[pl.ds(0, 255 * 16)] if ref is None else ref.at[pl.ds(0, 255)]
        pltpu.make_async_copy(ref, ref, send.at[n]).wait()
    gain_copy.wait()
    for copy in copies:
        copy.wait()


def exchange(frames, probe):
    wy, wx, perm, det = (jnp.asarray(t) for t in tables())
    hbm = pl.BlockSpec(memory_space=pl.ANY)
    dma = pltpu.SemaphoreType.DMA
    return pl.pallas_call(
        exchange_kernel,
        out_shape=(jax.ShapeDtypeStruct((2, 512, 1024), BF16), jax.ShapeDtypeStruct((2, 64, 1024), F32)),
        in_specs=[hbm] * 6,
        out_specs=(hbm, hbm),
        scratch_shapes=[
            pltpu.VMEM((512, 1024), BF16),
            pltpu.VMEM((2, 8, 128), F32),
            pltpu.VMEM((16, 2, 8, 128), F32),
            pltpu.VMEM((512, 1024), BF16),
            pltpu.VMEM((2, 256, 512), BF16),
            pltpu.VMEM((512, 512), BF16),
            pltpu.VMEM((4, 32, 1024), F32),
            pltpu.VMEM((4, 512, 128), F32),
            pltpu.VMEM((4096, 128), F32),
            pltpu.VMEM((2, 256, 8, 128), BF16),
            pltpu.VMEM((2, 256, 8, 128), BF16),
            pltpu.VMEM((4, 4, 128, 128), BF16),
            pltpu.VMEM((512, 512), BF16),
            pltpu.VMEM((4, 4, 256, 128), BF16),
            pltpu.VMEM((16, 256, 128), BF16),
            pltpu.VMEM((16, 32, 8, 128), BF16),
            pltpu.VMEM((4096, 128), BF16),
            pltpu.VMEM((2, 256, 8, 128), BF16),
            pltpu.VMEM((512, 1024), BF16),
            pltpu.VMEM((2, 1024, 1024), BF16),
            pltpu.VMEM((2, 1024, 1024), BF16),
            pltpu.VMEM((2, 64, 1024), F32),
            pltpu.VMEM((2, 64, 1024), F32),
            pltpu.VMEM((4, 512, 256), F32),
            pltpu.VMEM((4, 512, 256), F32),
            pltpu.VMEM((2, 512, 1024), BF16),
            dma((6,)), dma, dma, dma((5,)), dma((5,)), dma((3,)),
        ],
        compiler_params=pltpu.CompilerParams(collective_id=0, has_side_effects=True, vmem_limit_bytes=60 << 20),
    )(frames, probe, wy, wx, perm, det)


def quotient_kernel(spec, gain, out_re, out_im):
    row = lax.broadcasted_iota(jnp.int32, (8, 128), 0)

    @pl.loop(0, 8)
    def _(j):
        gains = []
        for c in range(2):
            tiles = []
            for t in range(4):
                first = jnp.broadcast_to(gain[c, pl.ds(16 * t + j, 1), :], (8, 128))
                second = jnp.broadcast_to(gain[c, pl.ds(16 * t + 8 + j, 1), :], (8, 128))
                tiles.append(jnp.where(row < 4, first, second))
            gains.append(jnp.concatenate(tiles, axis=0))
        g_re, g_im = gains
        for w in range(2):
            v = 2 * j + w
            rows = pl.ds(pl.multiple_of(v * 32, 32), 32)
            s_re, s_im = spec[0, rows, :].astype(F32), spec[1, rows, :].astype(F32)
            out_re[pl.ds(v, 32, stride=16), :] = s_re * g_re + s_im * g_im
            out_im[pl.ds(v, 32, stride=16), :] = s_im * g_re - s_re * g_im


def quotient(spec, gain):
    return pl.pallas_call(
        quotient_kernel,
        grid=(8,),
        out_shape=(jax.ShapeDtypeStruct((512, 1024), F32),) * 2,
        in_specs=[
            pl.BlockSpec((2, 512, 128), lambda n: (0, 0, n)),
            pl.BlockSpec((2, 64, 128), lambda n: (0, 0, n)),
        ],
        out_specs=(pl.BlockSpec((512, 128), lambda n: (0, n)),) * 2,
        compiler_params=pltpu.CompilerParams(vmem_limit_bytes=60 << 20),
    )(spec, gain)


def shards(frames, probe_wave):
    spec, gain = exchange(frames.reshape(512, PIX), probe_wave)
    real, imag = quotient(spec, gain)
    return real.reshape(32, 16, PIX), imag.reshape(32, 16, PIX)


def solution(mesh):
    return jax.shard_map(
        shards,
        mesh=mesh,
        in_specs=(P("grp", "mem", None), P(None, "mem", None)),
        out_specs=(P("mem", "grp", None), P("mem", "grp", None)),
        check_vma=False,
    )
```

```python
import math

import jax
import jax.numpy as jnp
import ml_dtypes
import numpy as np
from jax import lax
from jax.experimental import pallas as pl
from jax.experimental.pallas import tpu as pltpu
from jax.sharding import PartitionSpec as P

WIN = 32
SCAN_Y = 512
SCAN_X = 256
PIX = 1024
MESH = pl.DeviceIdType.MESH
F32 = jnp.float32
BF16 = jnp.bfloat16

wiener_floor = 0.5


def scan_table(length):
    positions = np.arange(length)
    phases = (positions[:, None] * positions[None, :]) % length
    angles = -2.0 * math.pi / length * phases
    factor = 1.0 / math.sqrt(length)
    real = (np.cos(angles) * factor).astype(np.float32).astype(ml_dtypes.bfloat16)
    imag = (np.sin(angles) * factor).astype(np.float32).astype(ml_dtypes.bfloat16)
    return real, imag


def tables():
    yr, yi = scan_table(SCAN_Y)
    wy = np.concatenate([yr, yi], axis=1)
    xr, xi = scan_table(SCAN_X)
    order = np.arange(SCAN_X).reshape(16, 8, 2).transpose(2, 0, 1).reshape(-1)
    xr, xi = xr[:, order], xi[:, order]
    wx = np.stack([np.concatenate([xr, -xi], axis=1), np.concatenate([xi, xr], axis=1)])
    perm = np.zeros((512, 512), ml_dtypes.bfloat16)
    src = np.arange(512)
    perm[src, (src // 32 % 4) * 128 + (src // 128) * 32 + src % 32] = 1
    rows = np.zeros((256, 256), ml_dtypes.bfloat16)
    dst = np.arange(256)
    rows[dst, (dst % 8) * 32 + dst // 8] = 1
    pos = np.arange(WIN)
    angle = 2.0 * math.pi / WIN * (pos[:, None] * pos[None, :] % WIN)
    cos, sin = np.cos(angle), np.sin(angle)
    det = np.stack(
        [np.repeat(cos, WIN, 1), np.repeat(sin, WIN, 1), np.tile(cos, (1, WIN)) / WIN, np.tile(sin, (1, WIN)) / WIN]
    ).astype(np.float32)
    return wy, wx, perm, rows, det


def dot(a, b):
    return jnp.dot(a, b, preferred_element_type=F32)


def arrange_frames(h, x, xs, ms, m1):
    for lt in range(4):
        xs[lt] = x[:, h * 512 + lt * 128 : h * 512 + (lt + 1) * 128].astype(F32)

    @pl.loop(0, 8)
    def _(x8):
        for dh in range(2):
            block = jnp.concatenate(
                [xs[k2 * 2 + dh, pl.ds(2 * x8 + x2, 32, stride=16), :] for k2 in range(2) for x2 in range(2)], axis=0
            )
            ms[pl.ds(dh * 1024 + x8, 128, stride=8), :] = block.T

    m1[h] = ms[0:2048, :].reshape(256, 8, 128).astype(BF16)


def detector_table(det, ddr, ddi):
    @pl.loop(0, 32)
    def _(ky):
        ca, sa = det[0, pl.ds(ky, 1), :], det[1, pl.ds(ky, 1), :]
        cb, sb = det[2], det[3]
        real = cb * ca - sb * sa
        imag = -(sb * ca + cb * sa)
        h = ky // 16
        upper = pl.multiple_of((ky % 16) * 32, 32)
        lower = pl.multiple_of(upper + 512, 32)
        ddr[h, pl.ds(upper, 32), :] = real.astype(BF16)
        ddr[h, pl.ds(lower, 32), :] = (-imag).astype(BF16)
        ddi[h, pl.ds(upper, 32), :] = imag.astype(BF16)
        ddi[h, pl.ds(lower, 32), :] = real.astype(BF16)


def probe_products(g, m, prb, pf):
    lane = lax.broadcasted_iota(jnp.int32, (8, 128), 1)
    row = lax.broadcasted_iota(jnp.int32, (8, 128), 0)
    group = lane // 32

    def flat(x, j):
        w = pltpu.roll(x, (128 - j) % 128, 1) if j else x
        y = w
        for q in range(1, 4):
            y = jnp.where(group == q, pltpu.roll(w, 32 * q, 1), y)
        return [jnp.sum(jnp.where(row == group + 4 * half, y, 0.0), axis=0, keepdims=True) for half in range(2)]

    base = []
    ext = []
    for c in range(2):
        tiles = []
        for q in range(4):
            tiles += flat(prb[q, c], 0)
        base.append([jnp.broadcast_to(t, (8, 128)) for t in tiles])
        tiles = []
        for q in range(5):
            x = pltpu.roll(prb[lax.rem(m + q, 16), c], lax.rem(128 - 8 * g, 128), 1)
            halves = [jnp.zeros((8, 128), F32)] * 2
            for j in range(8):
                sums = flat(x, j)
                halves = [jnp.where(row == j, jnp.broadcast_to(s, (8, 128)), h) for s, h in zip(sums, halves)]
            tiles += halves
        ext.append(tiles)
    for i in range(8):
        off, turn = i // 4, i % 4
        moved = []
        for c in range(2):
            if turn:
                rolled = [pltpu.roll(t, 128 - 32 * turn, 1) for t in ext[c]]
                moved.append([jnp.where(group < 4 - turn, rolled[t + off], rolled[t + off + 1]) for t in range(8)])
            else:
                moved.append([ext[c][t + off] for t in range(8)])
        for t in range(8):
            br, bi, mr, mi = base[0][t], base[1][t], moved[0][t], moved[1][t]
            h, at = t // 4, (t % 4) * 128
            pf[h, i * 8 : i * 8 + 8, at : at + 128] = br * mr + bi * mi
            pf[h, i * 8 : i * 8 + 8, 512 + at : 512 + at + 128] = bi * mr - br * mi


def wiener_gain(pf, ddr, ddi, chi, gain):
    left, right = pf[0].astype(BF16), pf[1].astype(BF16)
    chi_re = dot(left, ddr[0]) + dot(right, ddr[1])
    chi_im = dot(left, ddi[0]) + dot(right, ddi[1])
    scale = 1.0 / (chi_re * chi_re + chi_im * chi_im + wiener_floor)
    chi[0] = chi_re * scale
    chi[1] = chi_im * scale
    row = lax.broadcasted_iota(jnp.int32, (8, 1024), 0) // 2

    @pl.loop(0, 8)
    def _(i):
        for c in range(2):
            for half in range(2):
                tile = jnp.broadcast_to(chi[c, pl.ds(8 * i + 4 * half, 1), :], (8, 1024))
                for j in range(1, 4):
                    tile = jnp.where(row == j, chi[c, pl.ds(8 * i + 4 * half + j, 1), :], tile)
                gain[c, i, half] = tile


def scan_transform(h, r, rp, cst, f, store, wy, wx, perm):
    @pl.loop(0, 4)
    def _(j):
        parts = [r[h, pl.ds((4 * j + t) * 16, 16)].astype(F32).reshape(128, 128) for t in range(4)]
        moved = dot(jnp.concatenate(parts, axis=1).astype(BF16), perm[...]).astype(BF16)
        for s in range(4):
            rp[s, j] = moved[:, s * 128 : (s + 1) * 128]

    @pl.loop(0, 2)
    def _(k2):
        lhs = jnp.concatenate(
            [jnp.concatenate([rp[2 * k2 + x2, j] for j in range(4)], axis=1) for x2 in range(2)], axis=0
        )
        for c in range(2):
            cst[c * 256 : (c + 1) * 256, :] = dot(lhs, wy[:, c * 512 : (c + 1) * 512]).astype(BF16)
        for c in range(2):
            res = dot(wx[c], cst[...]).astype(BF16)
            for t in range(4):
                f[t, 2 * c + k2] = res[:, t * 128 : (t + 1) * 128]

    @pl.loop(0, 4)
    def _(t):
        lhs = jnp.concatenate([f[t, s] for s in range(4)], axis=1)
        res = dot(lhs, perm[...])
        for q in range(4):
            store(4 * t + q, res[:, q * 128 : (q + 1) * 128])


def gather_pixels(z, count, half, raw, low, swap):
    @pl.loop(0, 8)
    def _(v):
        first = v + 8 * half if count == 16 else v
        halves = [z[pl.ds(dh * 128 * count + first, 128, stride=count), :].T for dh in range(2)]
        turned = jnp.concatenate(halves, axis=1).astype(BF16)
        rows = jnp.concatenate([turned[s * 32 : (s + 1) * 32, :] for s in range(4)], axis=1)
        raw[pl.ds(pl.multiple_of(v * 32, 32), 32), :] = rows

    low[half * 256 : (half + 1) * 256, :] = dot(swap[...], raw[...]).astype(BF16)


def exchange_kernel(
    frames, probe, wy_h, wx_h, perm_h, swap_h, det_h, spec_out, gain_out,
    x, pv, prb, wy, wx, perm, swap, det, xs, z, m1, r, rp, cst, f, m2, m3, r2, r3, raw, low, ddr, ddi, pf, chi, gain, sre, sim, spec,
    load_sem, prb_send, prb_recv, send, recv, out_sem,
):
    g, m = lax.axis_index("grp"), lax.axis_index("mem")
    me = g * 16 + m

    px, core, py = g // 4, lax.rem(g, 2), lax.rem(m, 4)
    pz = lax.rem(g // 2, 2) * 4 + m // 4
    turns = []
    for dz in (4, 3, 5, 2, 6, 1, 7, 0):
        z1 = lax.rem(pz + dz, 8)
        turns.append(((z1 // 4) * 2, lax.rem(z1, 4) * 4))

    def to_all(act):
        @pl.loop(1, 32)
        def _(i):
            step = 32 - i
            a = lax.rem(px + lax.rem(step // 2, 4), 4) * 4 + lax.rem(core + lax.rem(step, 2), 2)
            b = lax.rem(py + step // 8, 4)
            for za, zb in turns:
                act(a + za, b + zb)

        for za, zb in turns[:-1]:
            act(px * 4 + core + za, py + zb)

    def push(n, src, dst, a, b):
        pltpu.make_async_remote_copy(
            src_ref=src, dst_ref=dst, send_sem=send.at[n], recv_sem=recv.at[n], device_id=(a, b), device_id_type=MESH
        ).start()

    def arrived(n, ref):
        pltpu.make_async_copy(ref, ref, recv.at[n]).wait()

    loads = [
        pltpu.make_async_copy(src, dst, load_sem.at[n])
        for n, (src, dst) in enumerate(
            ((frames, x), (probe, pv), (wy_h, wy), (wx_h, wx), (perm_h, perm), (swap_h, swap), (det_h, det))
        )
    ]
    for load in loads:
        load.start()
    barrier = pltpu.get_barrier_semaphore()
    to_all(lambda a, b: pl.semaphore_signal(barrier, inc=1, device_id=(a, b), device_id_type=MESH))

    loads[0].wait()
    loads[1].wait()
    for h in range(2):
        arrange_frames(h, x, xs, z, m1)
    pl.semaphore_wait(barrier, 255)

    for h in range(2):
        pltpu.make_async_copy(m1.at[h, me], r.at[h, me], recv.at[h]).start()
        to_all(lambda a, b: push(h, m1.at[h, a * 16 + b], r.at[h, me], a, b))
        if h == 0:
            pltpu.make_async_copy(pv, prb.at[m], prb_recv).start()

            @pl.loop(1, 16)
            def _(i):
                pltpu.make_async_remote_copy(
                    src_ref=pv, dst_ref=prb.at[m], send_sem=prb_send, recv_sem=prb_recv,
                    device_id=(g, lax.rem(m + i, 16)), device_id_type=MESH,
                ).start()

    for load in loads[2:]:
        load.wait()

    arrived(0, r.at[0])

    def store_first(b, tile):
        m2[b] = tile.astype(BF16)

    scan_transform(0, r, rp, cst, f, store_first, wy, wx, perm)
    here = pl.ds(pl.multiple_of(me * 16, 16), 16)
    pltpu.make_async_copy(m2.at[m, pl.ds(pl.multiple_of(g * 16, 16), 16)], r2.at[here], recv.at[2]).start()
    to_all(lambda a, b: push(2, m2.at[b, pl.ds(pl.multiple_of(a * 16, 16), 16)], r2.at[here], a, b))

    arrived(1, r.at[1])

    def store_second(b, tile):
        m3[b] = tile.reshape(32, 8, 128).astype(BF16)

    scan_transform(1, r, rp, cst, f, store_second, wy, wx, perm)
    for half in range(2):
        pltpu.make_async_copy(m3.at[m, 2 * g + half], r3.at[half, me], recv.at[3 + half]).start()
        to_all(lambda a, b: push(3 + half, m3.at[b, 2 * a + half], r3.at[half, me], a, b))

    detector_table(det, ddr, ddi)
    pltpu.make_async_copy(prb, prb, prb_recv).wait()
    probe_products(g, m, prb, pf)
    wiener_gain(pf, ddr, ddi, chi, gain)
    gain_copy = pltpu.make_async_copy(gain, gain_out, out_sem.at[0])
    gain_copy.start()

    arrived(2, r2)
    z[...] = r2[...].astype(F32)
    for half in range(2):
        gather_pixels(z, 16, half, raw, low, swap)

    @pl.loop(0, 4)
    def _(n):
        lanes = pl.ds(pl.multiple_of(n * 256, 256), 256)
        sre[n] = dot(low[...], ddr[0, :, lanes])
        sim[n] = dot(low[...], ddi[0, :, lanes])

    copies = []
    for half in range(2):
        arrived(3 + half, r3.at[half])
        z[0:2048, :] = r3[half].astype(F32).reshape(2048, 128)
        gather_pixels(z, 8, half, raw, low, swap)
        rows = slice(half * 256, (half + 1) * 256)

        @pl.loop(0, 4)
        def _(n):
            lanes = pl.ds(pl.multiple_of(n * 256, 256), 256)
            spec[0, rows, lanes] = (sre[n, rows, :] + dot(low[rows, :], ddr[1, :, lanes])).astype(BF16)
            spec[1, rows, lanes] = (sim[n, rows, :] + dot(low[rows, :], ddi[1, :, lanes])).astype(BF16)

        copies.append(pltpu.make_async_copy(spec.at[:, rows], spec_out.at[:, rows], out_sem.at[1 + half]))
        copies[-1].start()

    pltpu.make_async_copy(prb.at[pl.ds(0, 15)], prb.at[pl.ds(0, 15)], prb_send).wait()
    for n, ref in enumerate((r.at[0], r.at[1], None, r3.at[0], r3.at[1])):
        ref = r2.at[pl.ds(0, 255 * 16)] if ref is None else ref.at[pl.ds(0, 255)]
        pltpu.make_async_copy(ref, ref, send.at[n]).wait()
    gain_copy.wait()
    for copy in copies:
        copy.wait()


def exchange(frames, probe):
    wy, wx, perm, swap, det = (jnp.asarray(t) for t in tables())
    hbm = pl.BlockSpec(memory_space=pl.ANY)
    dma = pltpu.SemaphoreType.DMA
    return pl.pallas_call(
        exchange_kernel,
        out_shape=(jax.ShapeDtypeStruct((2, 512, 1024), BF16), jax.ShapeDtypeStruct((2, 8, 2, 8, 1024), F32)),
        in_specs=[hbm] * 7,
        out_specs=(hbm, hbm),
        scratch_shapes=[
            pltpu.VMEM((512, 1024), BF16),
            pltpu.VMEM((2, 8, 128), F32),
            pltpu.VMEM((16, 2, 8, 128), F32),
            pltpu.VMEM((512, 1024), BF16),
            pltpu.VMEM((2, 256, 512), BF16),
            pltpu.VMEM((512, 512), BF16),
            pltpu.VMEM((256, 256), BF16),
            pltpu.VMEM((4, 32, 1024), F32),
            pltpu.VMEM((4, 512, 128), F32),
            pltpu.VMEM((4096, 128), F32),
            pltpu.VMEM((2, 256, 8, 128), BF16),
            pltpu.VMEM((2, 256, 8, 128), BF16),
            pltpu.VMEM((4, 4, 128, 128), BF16),
            pltpu.VMEM((512, 512), BF16),
            pltpu.VMEM((4, 4, 256, 128), BF16),
            pltpu.VMEM((16, 256, 128), BF16),
            pltpu.VMEM((16, 32, 8, 128), BF16),
            pltpu.VMEM((4096, 128), BF16),
            pltpu.VMEM((2, 256, 8, 128), BF16),
            pltpu.VMEM((256, 1024), BF16),
            pltpu.VMEM((512, 1024), BF16),
            pltpu.VMEM((2, 1024, 1024), BF16),
            pltpu.VMEM((2, 1024, 1024), BF16),
            pltpu.VMEM((2, 64, 1024), F32),
            pltpu.VMEM((2, 64, 1024), F32),
            pltpu.VMEM((2, 8, 2, 8, 1024), F32),
            pltpu.VMEM((4, 512, 256), F32),
            pltpu.VMEM((4, 512, 256), F32),
            pltpu.VMEM((2, 512, 1024), BF16),
            dma((7,)), dma, dma, dma((5,)), dma((5,)), dma((3,)),
        ],
        compiler_params=pltpu.CompilerParams(collective_id=0, has_side_effects=True, vmem_limit_bytes=60 << 20),
    )(frames, probe, wy, wx, perm, swap, det)


def quotient_kernel(spec, gain, out_re, out_im):
    @pl.loop(0, 2)
    def _(i):
        for half in range(2):
            g_re, g_im = gain[0, i, half], gain[1, i, half]
            for w in range(4):
                u = 4 * i + w
                s_re, s_im = spec[0, half, u].astype(F32), spec[1, half, u].astype(F32)
                out_re[u, half * 8 : half * 8 + 8, :] = s_re * g_re + s_im * g_im
                out_im[u, half * 8 : half * 8 + 8, :] = s_im * g_re - s_re * g_im


def quotient(spec, gain):
    return pl.pallas_call(
        quotient_kernel,
        grid=(4,),
        out_shape=(jax.ShapeDtypeStruct((32, 16, 1024), F32),) * 2,
        in_specs=[
            pl.BlockSpec((2, 2, 8, 8, 1024), lambda n: (0, 0, n, 0, 0)),
            pl.BlockSpec((2, 2, 2, 8, 1024), lambda n: (0, n, 0, 0, 0)),
        ],
        out_specs=(pl.BlockSpec((8, 16, 1024), lambda n: (n, 0, 0)),) * 2,
        compiler_params=pltpu.CompilerParams(vmem_limit_bytes=60 << 20),
    )(spec.reshape(2, 2, 32, 8, 1024), gain)


def shards(frames, probe_wave):
    spec, gain = exchange(frames.reshape(512, PIX), probe_wave)
    return quotient(spec, gain)


def solution(mesh):
    return jax.shard_map(
        shards,
        mesh=mesh,
        in_specs=(P("grp", "mem", None), P(None, "mem", None)),
        out_specs=(P("mem", "grp", None), P("mem", "grp", None)),
        check_vma=False,
    )
```

```python
import math

import jax
import jax.numpy as jnp
import ml_dtypes
import numpy as np
from jax import lax
from jax.experimental import pallas as pl
from jax.experimental.pallas import tpu as pltpu
from jax.sharding import PartitionSpec as P

WIN = 32
SCAN_Y = 512
SCAN_X = 256
PIX = 1024
MESH = pl.DeviceIdType.MESH
F32 = jnp.float32
BF16 = jnp.bfloat16

wiener_floor = 0.5


def scan_table(length):
    positions = np.arange(length)
    phases = (positions[:, None] * positions[None, :]) % length
    angles = -2.0 * math.pi / length * phases
    factor = 1.0 / math.sqrt(length)
    real = (np.cos(angles) * factor).astype(np.float32).astype(ml_dtypes.bfloat16)
    imag = (np.sin(angles) * factor).astype(np.float32).astype(ml_dtypes.bfloat16)
    return real, imag


def tables():
    yr, yi = scan_table(SCAN_Y)
    wy = np.concatenate([yr, yi], axis=1)
    xr, xi = scan_table(SCAN_X)
    order = np.arange(SCAN_X).reshape(16, 8, 2).transpose(2, 0, 1).reshape(-1)
    xr, xi = xr[:, order], xi[:, order]
    wx = np.stack([np.concatenate([xr, -xi], axis=1), np.concatenate([xi, xr], axis=1)])
    perm = np.zeros((512, 512), ml_dtypes.bfloat16)
    src = np.arange(512)
    perm[src, (src // 32 % 4) * 128 + (src // 128) * 32 + src % 32] = 1
    rows = np.zeros((256, 256), ml_dtypes.bfloat16)
    dst = np.arange(256)
    rows[dst, (dst % 8) * 32 + dst // 8] = 1
    pos = np.arange(WIN)
    angle = 2.0 * math.pi / WIN * (pos[:, None] * pos[None, :] % WIN)
    cos, sin = np.cos(angle), np.sin(angle)
    det = np.stack(
        [np.repeat(cos, WIN, 1), np.repeat(sin, WIN, 1), np.tile(cos, (1, WIN)) / WIN, np.tile(sin, (1, WIN)) / WIN]
    ).astype(np.float32)
    return wy, wx, perm, rows, det


def dot(a, b):
    return jnp.dot(a, b, preferred_element_type=F32)


def arrange_frames(h, x, xs, ms, m1):
    for lt in range(4):
        xs[lt] = x[:, h * 512 + lt * 128 : h * 512 + (lt + 1) * 128].astype(F32)

    @pl.loop(0, 8)
    def _(x8):
        for dh in range(2):
            block = jnp.concatenate(
                [xs[k2 * 2 + dh, pl.ds(2 * x8 + x2, 32, stride=16), :] for k2 in range(2) for x2 in range(2)], axis=0
            )
            ms[pl.ds(dh * 1024 + x8, 128, stride=8), :] = block.T

    m1[h] = ms[0:2048, :].reshape(256, 8, 128).astype(BF16)


def detector_table(det, ddr, ddi):
    @pl.loop(0, 32)
    def _(ky):
        ca, sa = det[0, pl.ds(ky, 1), :], det[1, pl.ds(ky, 1), :]
        cb, sb = det[2], det[3]
        real = cb * ca - sb * sa
        imag = -(sb * ca + cb * sa)
        h = ky // 16
        upper = pl.multiple_of((ky % 16) * 32, 32)
        lower = pl.multiple_of(upper + 512, 32)
        ddr[h, pl.ds(upper, 32), :] = real.astype(BF16)
        ddr[h, pl.ds(lower, 32), :] = (-imag).astype(BF16)
        ddi[h, pl.ds(upper, 32), :] = imag.astype(BF16)
        ddi[h, pl.ds(lower, 32), :] = real.astype(BF16)


def probe_products(g, m, prb, pf):
    lane = lax.broadcasted_iota(jnp.int32, (8, 128), 1)
    row = lax.broadcasted_iota(jnp.int32, (8, 128), 0)
    group = lane // 32

    def flat(x, j):
        w = pltpu.roll(x, (128 - j) % 128, 1) if j else x
        y = w
        for q in range(1, 4):
            y = jnp.where(group == q, pltpu.roll(w, 32 * q, 1), y)
        return [jnp.sum(jnp.where(row == group + 4 * half, y, 0.0), axis=0, keepdims=True) for half in range(2)]

    base = []
    ext = []
    for c in range(2):
        tiles = []
        for q in range(4):
            tiles += flat(prb[q, c], 0)
        base.append([jnp.broadcast_to(t, (8, 128)) for t in tiles])
        tiles = []
        for q in range(5):
            x = pltpu.roll(prb[lax.rem(m + q, 16), c], lax.rem(128 - 8 * g, 128), 1)
            halves = [jnp.zeros((8, 128), F32)] * 2
            for j in range(8):
                sums = flat(x, j)
                halves = [jnp.where(row == j, jnp.broadcast_to(s, (8, 128)), h) for s, h in zip(sums, halves)]
            tiles += halves
        ext.append(tiles)
    for i in range(8):
        off, turn = i // 4, i % 4
        moved = []
        for c in range(2):
            if turn:
                rolled = [pltpu.roll(t, 128 - 32 * turn, 1) for t in ext[c]]
                moved.append([jnp.where(group < 4 - turn, rolled[t + off], rolled[t + off + 1]) for t in range(8)])
            else:
                moved.append([ext[c][t + off] for t in range(8)])
        for t in range(8):
            br, bi, mr, mi = base[0][t], base[1][t], moved[0][t], moved[1][t]
            h, at = t // 4, (t % 4) * 128
            pf[h, i * 8 : i * 8 + 8, at : at + 128] = br * mr + bi * mi
            pf[h, i * 8 : i * 8 + 8, 512 + at : 512 + at + 128] = bi * mr - br * mi


def wiener_gain(pf, ddr, ddi, chi, gain):
    left, right = pf[0].astype(BF16), pf[1].astype(BF16)
    chi_re = dot(left, ddr[0]) + dot(right, ddr[1])
    chi_im = dot(left, ddi[0]) + dot(right, ddi[1])
    scale = 1.0 / (chi_re * chi_re + chi_im * chi_im + wiener_floor)
    chi[0] = chi_re * scale
    chi[1] = chi_im * scale
    row = lax.broadcasted_iota(jnp.int32, (8, 1024), 0) // 2

    @pl.loop(0, 8)
    def _(i):
        for c in range(2):
            for half in range(2):
                tile = jnp.broadcast_to(chi[c, pl.ds(8 * i + 4 * half, 1), :], (8, 1024))
                for j in range(1, 4):
                    tile = jnp.where(row == j, chi[c, pl.ds(8 * i + 4 * half + j, 1), :], tile)
                gain[c, i, half] = tile


def scan_transform(h, r, rp, cst, f, store, wy, wx, perm):
    @pl.loop(0, 4)
    def _(j):
        parts = [r[h, pl.ds((4 * j + t) * 16, 16)].astype(F32).reshape(128, 128) for t in range(4)]
        moved = dot(jnp.concatenate(parts, axis=1).astype(BF16), perm[...]).astype(BF16)
        for s in range(4):
            rp[s, j] = moved[:, s * 128 : (s + 1) * 128]

    @pl.loop(0, 2)
    def _(k2):
        lhs = jnp.concatenate(
            [jnp.concatenate([rp[2 * k2 + x2, j] for j in range(4)], axis=1) for x2 in range(2)], axis=0
        )
        for c in range(2):
            cst[c * 256 : (c + 1) * 256, :] = dot(lhs, wy[:, c * 512 : (c + 1) * 512]).astype(BF16)
        for c in range(2):
            res = dot(wx[c], cst[...]).astype(BF16)
            for t in range(4):
                f[t, 2 * c + k2] = res[:, t * 128 : (t + 1) * 128]

    @pl.loop(0, 4)
    def _(t):
        lhs = jnp.concatenate([f[t, s] for s in range(4)], axis=1)
        res = dot(lhs, perm[...])
        for q in range(4):
            store(4 * t + q, res[:, q * 128 : (q + 1) * 128])


def gather_pixels(z, count, half, raw, low, swap, unroll):
    def gather(v):
        first = v + 8 * half if count == 16 else v
        halves = [z[pl.ds(dh * 128 * count + first, 128, stride=count), :].T for dh in range(2)]
        turned = jnp.concatenate(halves, axis=1).astype(BF16)
        rows = jnp.concatenate([turned[s * 32 : (s + 1) * 32, :] for s in range(4)], axis=1)
        raw[pl.ds(v * 32 if unroll else pl.multiple_of(v * 32, 32), 32), :] = rows

    if unroll:
        for v in range(8):
            gather(v)
    else:
        pl.loop(0, 8)(gather)
    low[half * 256 : (half + 1) * 256, :] = dot(swap[...], raw[...]).astype(BF16)


def exchange_kernel(
    frames, probe, wy_h, wx_h, perm_h, swap_h, det_h, spec, gain,
    x, pv, prb, wy, wx, perm, swap, det, xs, z, m1, r, rp, cst, f, m2, m3, r2, r3, raw, low, ddr, ddi, pf, chi, sre, sim,
    load_sem, prb_send, prb_recv, send, recv,
):
    g, m = lax.axis_index("grp"), lax.axis_index("mem")
    me = g * 16 + m

    px, core, py = g // 4, lax.rem(g, 2), lax.rem(m, 4)
    pz = lax.rem(g // 2, 2) * 4 + m // 4
    turns = []
    for dz in (4, 3, 5, 2, 6, 1, 7, 0):
        z1 = lax.rem(pz + dz, 8)
        turns.append(((z1 // 4) * 2, lax.rem(z1, 4) * 4))

    def to_all(act):
        @pl.loop(1, 32)
        def _(i):
            step = 32 - i
            a = lax.rem(px + lax.rem(step // 2, 4), 4) * 4 + lax.rem(core + lax.rem(step, 2), 2)
            b = lax.rem(py + step // 8, 4)
            for za, zb in turns:
                act(a + za, b + zb)

        for za, zb in turns[:-1]:
            act(px * 4 + core + za, py + zb)

    def push(n, src, dst, a, b):
        pltpu.make_async_remote_copy(
            src_ref=src, dst_ref=dst, send_sem=send.at[n], recv_sem=recv.at[n], device_id=(a, b), device_id_type=MESH
        ).start()

    def arrived(n, ref):
        pltpu.make_async_copy(ref, ref, recv.at[n]).wait()

    loads = [
        pltpu.make_async_copy(src, dst, load_sem.at[n])
        for n, (src, dst) in enumerate(
            ((frames, x), (probe, pv), (wy_h, wy), (wx_h, wx), (perm_h, perm), (swap_h, swap), (det_h, det))
        )
    ]
    for load in loads:
        load.start()
    barrier = pltpu.get_barrier_semaphore()
    to_all(lambda a, b: pl.semaphore_signal(barrier, inc=1, device_id=(a, b), device_id_type=MESH))

    loads[0].wait()
    loads[1].wait()
    for h in range(2):
        arrange_frames(h, x, xs, z, m1)
    pl.semaphore_wait(barrier, 255)

    for h in range(2):
        pltpu.make_async_copy(m1.at[h, me], r.at[h, me], recv.at[h]).start()
        to_all(lambda a, b: push(h, m1.at[h, a * 16 + b], r.at[h, me], a, b))
        if h == 0:
            pltpu.make_async_copy(pv, prb.at[m], prb_recv).start()

            @pl.loop(1, 16)
            def _(i):
                pltpu.make_async_remote_copy(
                    src_ref=pv, dst_ref=prb.at[m], send_sem=prb_send, recv_sem=prb_recv,
                    device_id=(g, lax.rem(m + i, 16)), device_id_type=MESH,
                ).start()

    for load in loads[2:]:
        load.wait()

    arrived(0, r.at[0])

    def store_first(b, tile):
        m2[b] = tile.astype(BF16)

    scan_transform(0, r, rp, cst, f, store_first, wy, wx, perm)
    here = pl.ds(pl.multiple_of(me * 16, 16), 16)
    pltpu.make_async_copy(m2.at[m, pl.ds(pl.multiple_of(g * 16, 16), 16)], r2.at[here], recv.at[2]).start()
    to_all(lambda a, b: push(2, m2.at[b, pl.ds(pl.multiple_of(a * 16, 16), 16)], r2.at[here], a, b))

    arrived(1, r.at[1])

    def store_second(b, tile):
        m3[b] = tile.reshape(32, 8, 128).astype(BF16)

    scan_transform(1, r, rp, cst, f, store_second, wy, wx, perm)
    for half in range(2):
        pltpu.make_async_copy(m3.at[m, 2 * g + half], r3.at[half, me], recv.at[3 + half]).start()
        to_all(lambda a, b: push(3 + half, m3.at[b, 2 * a + half], r3.at[half, me], a, b))

    detector_table(det, ddr, ddi)
    pltpu.make_async_copy(prb, prb, prb_recv).wait()
    probe_products(g, m, prb, pf)
    wiener_gain(pf, ddr, ddi, chi, gain)

    arrived(2, r2)
    z[...] = r2[...].astype(F32)
    for half in range(2):
        gather_pixels(z, 16, half, raw, low, swap, False)

    @pl.loop(0, 4)
    def _(n):
        lanes = pl.ds(pl.multiple_of(n * 256, 256), 256)
        sre[n] = dot(low[...], ddr[0, :, lanes])
        sim[n] = dot(low[...], ddi[0, :, lanes])

    for half in range(2):
        arrived(3 + half, r3.at[half])
        z[0:2048, :] = r3[half].astype(F32).reshape(2048, 128)
        gather_pixels(z, 8, half, raw, low, swap, half == 1)
        rows = slice(half * 256, (half + 1) * 256)

        for n in range(4):
            lanes = slice(n * 256, (n + 1) * 256)
            spec[0, rows, lanes] = (sre[n, rows, :] + dot(low[rows, :], ddr[1, :, lanes])).astype(BF16)
            spec[1, rows, lanes] = (sim[n, rows, :] + dot(low[rows, :], ddi[1, :, lanes])).astype(BF16)


    pltpu.make_async_copy(prb.at[pl.ds(0, 15)], prb.at[pl.ds(0, 15)], prb_send).wait()
    for n, ref in enumerate((r.at[0], r.at[1], None, r3.at[0], r3.at[1])):
        ref = r2.at[pl.ds(0, 255 * 16)] if ref is None else ref.at[pl.ds(0, 255)]
        pltpu.make_async_copy(ref, ref, send.at[n]).wait()


def exchange(frames, probe):
    wy, wx, perm, swap, det = (jnp.asarray(t) for t in tables())
    hbm = pl.BlockSpec(memory_space=pl.ANY)
    vmem = pl.BlockSpec(memory_space=pltpu.VMEM)
    dma = pltpu.SemaphoreType.DMA
    return pl.pallas_call(
        exchange_kernel,
        out_shape=(pltpu.VMEM((2, 512, 1024), BF16), pltpu.VMEM((2, 8, 2, 8, 1024), F32)),
        in_specs=[hbm] * 7,
        out_specs=(vmem, vmem),
        scratch_shapes=[
            pltpu.VMEM((512, 1024), BF16),
            pltpu.VMEM((2, 8, 128), F32),
            pltpu.VMEM((16, 2, 8, 128), F32),
            pltpu.VMEM((512, 1024), BF16),
            pltpu.VMEM((2, 256, 512), BF16),
            pltpu.VMEM((512, 512), BF16),
            pltpu.VMEM((256, 256), BF16),
            pltpu.VMEM((4, 32, 1024), F32),
            pltpu.VMEM((4, 512, 128), F32),
            pltpu.VMEM((4096, 128), F32),
            pltpu.VMEM((2, 256, 8, 128), BF16),
            pltpu.VMEM((2, 256, 8, 128), BF16),
            pltpu.VMEM((4, 4, 128, 128), BF16),
            pltpu.VMEM((512, 512), BF16),
            pltpu.VMEM((4, 4, 256, 128), BF16),
            pltpu.VMEM((16, 256, 128), BF16),
            pltpu.VMEM((16, 32, 8, 128), BF16),
            pltpu.VMEM((4096, 128), BF16),
            pltpu.VMEM((2, 256, 8, 128), BF16),
            pltpu.VMEM((256, 1024), BF16),
            pltpu.VMEM((512, 1024), BF16),
            pltpu.VMEM((2, 1024, 1024), BF16),
            pltpu.VMEM((2, 1024, 1024), BF16),
            pltpu.VMEM((2, 64, 1024), F32),
            pltpu.VMEM((2, 64, 1024), F32),
            pltpu.VMEM((4, 512, 256), F32),
            pltpu.VMEM((4, 512, 256), F32),
            dma((7,)), dma, dma, dma((5,)), dma((5,)),
        ],
        compiler_params=pltpu.CompilerParams(collective_id=0, has_side_effects=True, vmem_limit_bytes=52 << 20),
    )(frames, probe, wy, wx, perm, swap, det)


def quotient_kernel(spec, gain, out_re, out_im):
    n = pl.program_id(0)
    for half in range(2):
        g_re, g_im = gain[0, n, half], gain[1, n, half]
        rows = pl.ds(pl.multiple_of(half * 256 + n * 32, 32), 32)
        s_re, s_im = spec[0, rows, :].astype(F32), spec[1, rows, :].astype(F32)
        for u in range(4):
            a, b = s_re[u * 8 : u * 8 + 8, :], s_im[u * 8 : u * 8 + 8, :]
            out_re[u, half * 8 : half * 8 + 8, :] = a * g_re + b * g_im
            out_im[u, half * 8 : half * 8 + 8, :] = b * g_re - a * g_im


def quotient(spec, gain):
    vmem = pl.BlockSpec(memory_space=pltpu.VMEM)
    return pl.pallas_call(
        quotient_kernel,
        grid=(8,),
        out_shape=(jax.ShapeDtypeStruct((32, 16, 1024), F32),) * 2,
        in_specs=[vmem, vmem],
        out_specs=(pl.BlockSpec((4, 16, 1024), lambda n: (n, 0, 0)),) * 2,
        compiler_params=pltpu.CompilerParams(vmem_limit_bytes=16 << 20),
    )(spec, gain)


def shards(frames, probe_wave):
    spec, gain = exchange(frames.reshape(512, PIX), probe_wave)
    return quotient(spec, gain)


def solution(mesh):
    return jax.shard_map(
        shards,
        mesh=mesh,
        in_specs=(P("grp", "mem", None), P(None, "mem", None)),
        out_specs=(P("mem", "grp", None), P("mem", "grp", None)),
        check_vma=False,
    )
```

```python
import math

import jax
import jax.numpy as jnp
import ml_dtypes
import numpy as np
from jax import lax
from jax.experimental import pallas as pl
from jax.experimental.pallas import tpu as pltpu
from jax.sharding import PartitionSpec as P

WIN = 32
SCAN_Y = 512
SCAN_X = 256
PIX = 1024
MESH = pl.DeviceIdType.MESH
F32 = jnp.float32
BF16 = jnp.bfloat16

wiener_floor = 0.5


def scan_table(length):
    positions = np.arange(length)
    phases = (positions[:, None] * positions[None, :]) % length
    angles = -2.0 * math.pi / length * phases
    factor = 1.0 / math.sqrt(length)
    real = (np.cos(angles) * factor).astype(np.float32).astype(ml_dtypes.bfloat16)
    imag = (np.sin(angles) * factor).astype(np.float32).astype(ml_dtypes.bfloat16)
    return real, imag


def tables():
    yr, yi = scan_table(SCAN_Y)
    wy = np.concatenate([yr, yi], axis=1)
    xr, xi = scan_table(SCAN_X)
    order = np.arange(SCAN_X).reshape(16, 8, 2).transpose(2, 0, 1).reshape(-1)
    xr, xi = xr[:, order], xi[:, order]
    wx = np.stack([np.concatenate([xr, -xi], axis=1), np.concatenate([xi, xr], axis=1)])
    perm = np.zeros((512, 512), ml_dtypes.bfloat16)
    src = np.arange(512)
    perm[src, (src // 32 % 4) * 128 + (src // 128) * 32 + src % 32] = 1
    rows = np.zeros((256, 256), ml_dtypes.bfloat16)
    dst = np.arange(256)
    rows[dst, (dst % 8) * 32 + dst // 8] = 1
    pos = np.arange(WIN)
    angle = 2.0 * math.pi / WIN * (pos[:, None] * pos[None, :] % WIN)
    cos, sin = np.cos(angle), np.sin(angle)
    det = np.stack(
        [np.repeat(cos, WIN, 1), np.repeat(sin, WIN, 1), np.tile(cos, (1, WIN)) / WIN, np.tile(sin, (1, WIN)) / WIN]
    ).astype(np.float32)
    return wy, wx, perm, rows, det


def dot(a, b):
    return jnp.dot(a, b, preferred_element_type=F32)


def arrange_frames(h, x, xs, ms, m1):
    for lt in range(4):
        xs[lt] = x[:, h * 512 + lt * 128 : h * 512 + (lt + 1) * 128].astype(F32)

    @pl.loop(0, 8)
    def _(x8):
        for dh in range(2):
            block = jnp.concatenate(
                [xs[k2 * 2 + dh, pl.ds(2 * x8 + x2, 32, stride=16), :] for k2 in range(2) for x2 in range(2)], axis=0
            )
            ms[pl.ds(dh * 1024 + x8, 128, stride=8), :] = block.T

    m1[h] = ms[0:2048, :].reshape(256, 8, 128).astype(BF16)


def detector_table(det, ddr, ddi):
    @pl.loop(0, 32)
    def _(ky):
        ca, sa = det[0, pl.ds(ky, 1), :], det[1, pl.ds(ky, 1), :]
        cb, sb = det[2], det[3]
        real = cb * ca - sb * sa
        imag = -(sb * ca + cb * sa)
        h = ky // 16
        upper = pl.multiple_of((ky % 16) * 32, 32)
        lower = pl.multiple_of(upper + 512, 32)
        ddr[h, pl.ds(upper, 32), :] = real.astype(BF16)
        ddr[h, pl.ds(lower, 32), :] = (-imag).astype(BF16)
        ddi[h, pl.ds(upper, 32), :] = imag.astype(BF16)
        ddi[h, pl.ds(lower, 32), :] = real.astype(BF16)


def probe_products(g, m, prb, pf):
    lane = lax.broadcasted_iota(jnp.int32, (8, 128), 1)
    row = lax.broadcasted_iota(jnp.int32, (8, 128), 0)
    group = lane // 32

    def flat(x, j):
        w = pltpu.roll(x, (128 - j) % 128, 1) if j else x
        y = w
        for q in range(1, 4):
            y = jnp.where(group == q, pltpu.roll(w, 32 * q, 1), y)
        return [jnp.sum(jnp.where(row == group + 4 * half, y, 0.0), axis=0, keepdims=True) for half in range(2)]

    base = []
    ext = []
    for c in range(2):
        tiles = []
        for q in range(4):
            tiles += flat(prb[q, c], 0)
        base.append([jnp.broadcast_to(t, (8, 128)) for t in tiles])
        tiles = []
        for q in range(5):
            x = pltpu.roll(prb[lax.rem(m + q, 16), c], lax.rem(128 - 8 * g, 128), 1)
            halves = [jnp.zeros((8, 128), F32)] * 2
            for j in range(8):
                sums = flat(x, j)
                halves = [jnp.where(row == j, jnp.broadcast_to(s, (8, 128)), h) for s, h in zip(sums, halves)]
            tiles += halves
        ext.append(tiles)
    for i in range(8):
        off, turn = i // 4, i % 4
        moved = []
        for c in range(2):
            if turn:
                rolled = [pltpu.roll(t, 128 - 32 * turn, 1) for t in ext[c]]
                moved.append([jnp.where(group < 4 - turn, rolled[t + off], rolled[t + off + 1]) for t in range(8)])
            else:
                moved.append([ext[c][t + off] for t in range(8)])
        for t in range(8):
            br, bi, mr, mi = base[0][t], base[1][t], moved[0][t], moved[1][t]
            h, at = t // 4, (t % 4) * 128
            pf[h, i * 8 : i * 8 + 8, at : at + 128] = br * mr + bi * mi
            pf[h, i * 8 : i * 8 + 8, 512 + at : 512 + at + 128] = bi * mr - br * mi


def wiener_gain(pf, ddr, ddi, chi, gain):
    left, right = pf[0].astype(BF16), pf[1].astype(BF16)
    chi_re = dot(left, ddr[0]) + dot(right, ddr[1])
    chi_im = dot(left, ddi[0]) + dot(right, ddi[1])
    scale = 1.0 / (chi_re * chi_re + chi_im * chi_im + wiener_floor)
    chi[0] = chi_re * scale
    chi[1] = chi_im * scale
    row = lax.broadcasted_iota(jnp.int32, (8, 1024), 0) // 2

    @pl.loop(0, 8)
    def _(i):
        for c in range(2):
            for half in range(2):
                tile = jnp.broadcast_to(chi[c, pl.ds(8 * i + 4 * half, 1), :], (8, 1024))
                for j in range(1, 4):
                    tile = jnp.where(row == j, chi[c, pl.ds(8 * i + 4 * half + j, 1), :], tile)
                gain[c, i, half] = tile


def scan_transform(h, r, rp, cst, f, store, wy, wx, perm):
    @pl.loop(0, 4)
    def _(j):
        parts = [r[h, pl.ds((4 * j + t) * 16, 16)].astype(F32).reshape(128, 128) for t in range(4)]
        moved = dot(jnp.concatenate(parts, axis=1).astype(BF16), perm[...]).astype(BF16)
        for s in range(4):
            rp[s, j] = moved[:, s * 128 : (s + 1) * 128]

    @pl.loop(0, 2)
    def _(k2):
        lhs = jnp.concatenate(
            [jnp.concatenate([rp[2 * k2 + x2, j] for j in range(4)], axis=1) for x2 in range(2)], axis=0
        )
        for c in range(2):
            cst[c * 256 : (c + 1) * 256, :] = dot(lhs, wy[:, c * 512 : (c + 1) * 512]).astype(BF16)
        for c in range(2):
            res = dot(wx[c], cst[...]).astype(BF16)
            for t in range(4):
                f[t, 2 * c + k2] = res[:, t * 128 : (t + 1) * 128]

    @pl.loop(0, 4)
    def _(t):
        lhs = jnp.concatenate([f[t, s] for s in range(4)], axis=1)
        res = dot(lhs, perm[...])
        for q in range(4):
            store(4 * t + q, res[:, q * 128 : (q + 1) * 128])


def gather_pixels(z, count, half, raw, low, swap, unroll):
    def gather(v):
        first = v + 8 * half if count == 16 else v
        halves = [z[pl.ds(dh * 128 * count + first, 128, stride=count), :].T for dh in range(2)]
        turned = jnp.concatenate(halves, axis=1).astype(BF16)
        rows = jnp.concatenate([turned[s * 32 : (s + 1) * 32, :] for s in range(4)], axis=1)
        raw[pl.ds(v * 32 if unroll else pl.multiple_of(v * 32, 32), 32), :] = rows

    if unroll:
        for v in range(8):
            gather(v)
    else:
        pl.loop(0, 8)(gather)
    low[half * 256 : (half + 1) * 256, :] = dot(swap[...], raw[...]).astype(BF16)


def exchange_kernel(
    frames, probe, wy_h, wx_h, perm_h, swap_h, det_h, spec, gain,
    x, pv, prb, wy, wx, perm, swap, det, xs, z, m1, r, rp, cst, f, m2, m3, r2, r3, raw, low, ddr, ddi, pf, chi, sre, sim,
    load_sem, prb_send, prb_recv, send, recv,
):
    g, m = lax.axis_index("grp"), lax.axis_index("mem")
    me = g * 16 + m

    px, core, py = g // 4, lax.rem(g, 2), lax.rem(m, 4)
    pz = lax.rem(g // 2, 2) * 4 + m // 4
    turns = []
    for dz in (4, 3, 5, 2, 6, 1, 7, 0):
        z1 = lax.rem(pz + dz, 8)
        turns.append(((z1 // 4) * 2, lax.rem(z1, 4) * 4))

    def to_all(act):
        @pl.loop(1, 32)
        def _(i):
            step = 32 - i
            a = lax.rem(px + lax.rem(step // 2, 4), 4) * 4 + lax.rem(core + lax.rem(step, 2), 2)
            b = lax.rem(py + step // 8, 4)
            for za, zb in turns:
                act(a + za, b + zb)

        for za, zb in turns[:-1]:
            act(px * 4 + core + za, py + zb)

    def push(n, src, dst, a, b):
        pltpu.make_async_remote_copy(
            src_ref=src, dst_ref=dst, send_sem=send.at[n], recv_sem=recv.at[n], device_id=(a, b), device_id_type=MESH
        ).start()

    def arrived(n, ref):
        pltpu.make_async_copy(ref, ref, recv.at[n]).wait()

    loads = [
        pltpu.make_async_copy(src, dst, load_sem.at[n])
        for n, (src, dst) in enumerate(
            ((frames, x), (probe, pv), (wy_h, wy), (wx_h, wx), (perm_h, perm), (swap_h, swap), (det_h, det))
        )
    ]
    for load in loads:
        load.start()
    barrier = pltpu.get_barrier_semaphore()
    to_all(lambda a, b: pl.semaphore_signal(barrier, inc=1, device_id=(a, b), device_id_type=MESH))

    loads[0].wait()
    loads[1].wait()
    arrange_frames(0, x, xs, z, m1)
    pl.semaphore_wait(barrier, 255)

    for h in range(2):
        if h == 1:
            arrange_frames(1, x, xs, z, m1)
        pltpu.make_async_copy(m1.at[h, me], r.at[h, me], recv.at[h]).start()
        to_all(lambda a, b: push(h, m1.at[h, a * 16 + b], r.at[h, me], a, b))
        if h == 0:
            pltpu.make_async_copy(pv, prb.at[m], prb_recv).start()

            @pl.loop(1, 16)
            def _(i):
                pltpu.make_async_remote_copy(
                    src_ref=pv, dst_ref=prb.at[m], send_sem=prb_send, recv_sem=prb_recv,
                    device_id=(g, lax.rem(m + i, 16)), device_id_type=MESH,
                ).start()

    for load in loads[2:]:
        load.wait()

    arrived(0, r.at[0])

    def store_first(b, tile):
        m2[b] = tile.astype(BF16)

    scan_transform(0, r, rp, cst, f, store_first, wy, wx, perm)
    here = pl.ds(pl.multiple_of(me * 16, 16), 16)
    pltpu.make_async_copy(m2.at[m, pl.ds(pl.multiple_of(g * 16, 16), 16)], r2.at[here], recv.at[2]).start()
    to_all(lambda a, b: push(2, m2.at[b, pl.ds(pl.multiple_of(a * 16, 16), 16)], r2.at[here], a, b))

    arrived(1, r.at[1])

    def store_second(b, tile):
        m3[b] = tile.reshape(32, 8, 128).astype(BF16)

    scan_transform(1, r, rp, cst, f, store_second, wy, wx, perm)
    for half in range(2):
        pltpu.make_async_copy(m3.at[m, 2 * g + half], r3.at[half, me], recv.at[3 + half]).start()
        to_all(lambda a, b: push(3 + half, m3.at[b, 2 * a + half], r3.at[half, me], a, b))

    detector_table(det, ddr, ddi)
    pltpu.make_async_copy(prb, prb, prb_recv).wait()
    probe_products(g, m, prb, pf)
    wiener_gain(pf, ddr, ddi, chi, gain)

    arrived(2, r2)
    z[...] = r2[...].astype(F32)
    for half in range(2):
        gather_pixels(z, 16, half, raw, low, swap, False)

    @pl.loop(0, 4)
    def _(n):
        lanes = pl.ds(pl.multiple_of(n * 256, 256), 256)
        sre[n] = dot(low[...], ddr[0, :, lanes])
        sim[n] = dot(low[...], ddi[0, :, lanes])

    for half in range(2):
        arrived(3 + half, r3.at[half])
        z[0:2048, :] = r3[half].astype(F32).reshape(2048, 128)
        gather_pixels(z, 8, half, raw, low, swap, half == 1)
        rows = slice(half * 256, (half + 1) * 256)

        for n in range(4):
            lanes = slice(n * 256, (n + 1) * 256)
            spec[0, rows, lanes] = (sre[n, rows, :] + dot(low[rows, :], ddr[1, :, lanes])).astype(BF16)
            spec[1, rows, lanes] = (sim[n, rows, :] + dot(low[rows, :], ddi[1, :, lanes])).astype(BF16)


    pltpu.make_async_copy(prb.at[pl.ds(0, 15)], prb.at[pl.ds(0, 15)], prb_send).wait()
    for n, ref in enumerate((r.at[0], r.at[1], None, r3.at[0], r3.at[1])):
        ref = r2.at[pl.ds(0, 255 * 16)] if ref is None else ref.at[pl.ds(0, 255)]
        pltpu.make_async_copy(ref, ref, send.at[n]).wait()


def exchange(frames, probe):
    wy, wx, perm, swap, det = (jnp.asarray(t) for t in tables())
    hbm = pl.BlockSpec(memory_space=pl.ANY)
    vmem = pl.BlockSpec(memory_space=pltpu.VMEM)
    dma = pltpu.SemaphoreType.DMA
    return pl.pallas_call(
        exchange_kernel,
        out_shape=(pltpu.VMEM((2, 512, 1024), BF16), pltpu.VMEM((2, 8, 2, 8, 1024), F32)),
        in_specs=[hbm] * 7,
        out_specs=(vmem, vmem),
        scratch_shapes=[
            pltpu.VMEM((512, 1024), BF16),
            pltpu.VMEM((2, 8, 128), F32),
            pltpu.VMEM((16, 2, 8, 128), F32),
            pltpu.VMEM((512, 1024), BF16),
            pltpu.VMEM((2, 256, 512), BF16),
            pltpu.VMEM((512, 512), BF16),
            pltpu.VMEM((256, 256), BF16),
            pltpu.VMEM((4, 32, 1024), F32),
            pltpu.VMEM((4, 512, 128), F32),
            pltpu.VMEM((4096, 128), F32),
            pltpu.VMEM((2, 256, 8, 128), BF16),
            pltpu.VMEM((2, 256, 8, 128), BF16),
            pltpu.VMEM((4, 4, 128, 128), BF16),
            pltpu.VMEM((512, 512), BF16),
            pltpu.VMEM((4, 4, 256, 128), BF16),
            pltpu.VMEM((16, 256, 128), BF16),
            pltpu.VMEM((16, 32, 8, 128), BF16),
            pltpu.VMEM((4096, 128), BF16),
            pltpu.VMEM((2, 256, 8, 128), BF16),
            pltpu.VMEM((256, 1024), BF16),
            pltpu.VMEM((512, 1024), BF16),
            pltpu.VMEM((2, 1024, 1024), BF16),
            pltpu.VMEM((2, 1024, 1024), BF16),
            pltpu.VMEM((2, 64, 1024), F32),
            pltpu.VMEM((2, 64, 1024), F32),
            pltpu.VMEM((4, 512, 256), F32),
            pltpu.VMEM((4, 512, 256), F32),
            dma((7,)), dma, dma, dma((5,)), dma((5,)),
        ],
        compiler_params=pltpu.CompilerParams(collective_id=0, has_side_effects=True, vmem_limit_bytes=52 << 20),
    )(frames, probe, wy, wx, perm, swap, det)


def quotient_kernel(spec, gain, out_re, out_im):
    n = pl.program_id(0)
    for half in range(2):
        g_re, g_im = gain[0, n, half], gain[1, n, half]
        rows = pl.ds(pl.multiple_of(half * 256 + n * 32, 32), 32)
        s_re, s_im = spec[0, rows, :].astype(F32), spec[1, rows, :].astype(F32)
        for u in range(4):
            a, b = s_re[u * 8 : u * 8 + 8, :], s_im[u * 8 : u * 8 + 8, :]
            out_re[u, half * 8 : half * 8 + 8, :] = a * g_re + b * g_im
            out_im[u, half * 8 : half * 8 + 8, :] = b * g_re - a * g_im


def quotient(spec, gain):
    vmem = pl.BlockSpec(memory_space=pltpu.VMEM)
    return pl.pallas_call(
        quotient_kernel,
        grid=(8,),
        out_shape=(jax.ShapeDtypeStruct((32, 16, 1024), F32),) * 2,
        in_specs=[vmem, vmem],
        out_specs=(pl.BlockSpec((4, 16, 1024), lambda n: (n, 0, 0)),) * 2,
        compiler_params=pltpu.CompilerParams(vmem_limit_bytes=16 << 20),
    )(spec, gain)


def shards(frames, probe_wave):
    spec, gain = exchange(frames.reshape(512, PIX), probe_wave)
    return quotient(spec, gain)


def solution(mesh):
    return jax.shard_map(
        shards,
        mesh=mesh,
        in_specs=(P("grp", "mem", None), P(None, "mem", None)),
        out_specs=(P("mem", "grp", None), P("mem", "grp", None)),
        check_vma=False,
    )
```

```python
import math

import jax
import jax.numpy as jnp
import ml_dtypes
import numpy as np
from jax import lax
from jax.experimental import pallas as pl
from jax.experimental.pallas import tpu as pltpu
from jax.sharding import PartitionSpec as P

WIN = 32
SCAN_Y = 512
SCAN_X = 256
PIX = 1024
MESH = pl.DeviceIdType.MESH
F32 = jnp.float32
BF16 = jnp.bfloat16

wiener_floor = 0.5


def scan_table(length):
    positions = np.arange(length)
    phases = (positions[:, None] * positions[None, :]) % length
    angles = -2.0 * math.pi / length * phases
    factor = 1.0 / math.sqrt(length)
    real = (np.cos(angles) * factor).astype(np.float32).astype(ml_dtypes.bfloat16)
    imag = (np.sin(angles) * factor).astype(np.float32).astype(ml_dtypes.bfloat16)
    return real, imag


def tables():
    yr, yi = scan_table(SCAN_Y)
    wy = np.concatenate([yr, yi], axis=1)
    xr, xi = scan_table(SCAN_X)
    order = np.arange(SCAN_X).reshape(16, 8, 2).transpose(2, 0, 1).reshape(-1)
    xr, xi = xr[:, order], xi[:, order]
    wx = np.stack([np.concatenate([xr, -xi], axis=1), np.concatenate([xi, xr], axis=1)])
    perm = np.zeros((512, 512), ml_dtypes.bfloat16)
    src = np.arange(512)
    perm[src, (src // 32 % 4) * 128 + (src // 128) * 32 + src % 32] = 1
    rows = np.zeros((256, 256), ml_dtypes.bfloat16)
    dst = np.arange(256)
    rows[dst, (dst % 8) * 32 + dst // 8] = 1
    pos = np.arange(WIN)
    angle = 2.0 * math.pi / WIN * (pos[:, None] * pos[None, :] % WIN)
    cos, sin = np.cos(angle), np.sin(angle)
    det = np.stack(
        [np.repeat(cos, WIN, 1), np.repeat(sin, WIN, 1), np.tile(cos, (1, WIN)) / WIN, np.tile(sin, (1, WIN)) / WIN]
    ).astype(np.float32)
    return wy, wx, perm, rows, det


def dot(a, b):
    return jnp.dot(a, b, preferred_element_type=F32)


def arrange_frames(h, x, xs, ms, m1):
    for lt in range(4):
        xs[lt] = x[:, h * 512 + lt * 128 : h * 512 + (lt + 1) * 128].astype(F32)

    @pl.loop(0, 8)
    def _(x8):
        for dh in range(2):
            block = jnp.concatenate(
                [xs[k2 * 2 + dh, pl.ds(2 * x8 + x2, 32, stride=16), :] for k2 in range(2) for x2 in range(2)], axis=0
            )
            ms[pl.ds(dh * 1024 + x8, 128, stride=8), :] = block.T

    m1[h] = ms[0:2048, :].reshape(256, 8, 128).astype(BF16)


def detector_table(det, ddr, ddi):
    @pl.loop(0, 32)
    def _(ky):
        ca, sa = det[0, pl.ds(ky, 1), :], det[1, pl.ds(ky, 1), :]
        cb, sb = det[2], det[3]
        real = cb * ca - sb * sa
        imag = -(sb * ca + cb * sa)
        h = ky // 16
        upper = pl.multiple_of((ky % 16) * 32, 32)
        lower = pl.multiple_of(upper + 512, 32)
        ddr[h, pl.ds(upper, 32), :] = real.astype(BF16)
        ddr[h, pl.ds(lower, 32), :] = (-imag).astype(BF16)
        ddi[h, pl.ds(upper, 32), :] = imag.astype(BF16)
        ddi[h, pl.ds(lower, 32), :] = real.astype(BF16)


def probe_products(g, m, prb, pf):
    lane = lax.broadcasted_iota(jnp.int32, (8, 128), 1)
    row = lax.broadcasted_iota(jnp.int32, (8, 128), 0)
    group = lane // 32

    def flat(x, j):
        w = pltpu.roll(x, (128 - j) % 128, 1) if j else x
        y = w
        for q in range(1, 4):
            y = jnp.where(group == q, pltpu.roll(w, 32 * q, 1), y)
        return [jnp.sum(jnp.where(row == group + 4 * half, y, 0.0), axis=0, keepdims=True) for half in range(2)]

    base = []
    ext = []
    for c in range(2):
        tiles = []
        for q in range(4):
            tiles += flat(prb[q, c], 0)
        base.append([jnp.broadcast_to(t, (8, 128)) for t in tiles])
        tiles = []
        for q in range(5):
            x = pltpu.roll(prb[lax.rem(m + q, 16), c], lax.rem(128 - 8 * g, 128), 1)
            halves = [jnp.zeros((8, 128), F32)] * 2
            for j in range(8):
                sums = flat(x, j)
                halves = [jnp.where(row == j, jnp.broadcast_to(s, (8, 128)), h) for s, h in zip(sums, halves)]
            tiles += halves
        ext.append(tiles)
    for i in range(8):
        off, turn = i // 4, i % 4
        moved = []
        for c in range(2):
            if turn:
                rolled = [pltpu.roll(t, 128 - 32 * turn, 1) for t in ext[c]]
                moved.append([jnp.where(group < 4 - turn, rolled[t + off], rolled[t + off + 1]) for t in range(8)])
            else:
                moved.append([ext[c][t + off] for t in range(8)])
        for t in range(8):
            br, bi, mr, mi = base[0][t], base[1][t], moved[0][t], moved[1][t]
            h, at = t // 4, (t % 4) * 128
            pf[h, i * 8 : i * 8 + 8, at : at + 128] = br * mr + bi * mi
            pf[h, i * 8 : i * 8 + 8, 512 + at : 512 + at + 128] = bi * mr - br * mi


def wiener_gain(pf, ddr, ddi, chi, gain):
    left, right = pf[0].astype(BF16), pf[1].astype(BF16)
    chi_re = dot(left, ddr[0]) + dot(right, ddr[1])
    chi_im = dot(left, ddi[0]) + dot(right, ddi[1])
    scale = 1.0 / (chi_re * chi_re + chi_im * chi_im + wiener_floor)
    chi[0] = chi_re * scale
    chi[1] = chi_im * scale
    row = lax.broadcasted_iota(jnp.int32, (8, 1024), 0) // 2

    @pl.loop(0, 8)
    def _(i):
        for c in range(2):
            for half in range(2):
                tile = jnp.broadcast_to(chi[c, pl.ds(8 * i + 4 * half, 1), :], (8, 1024))
                for j in range(1, 4):
                    tile = jnp.where(row == j, chi[c, pl.ds(8 * i + 4 * half + j, 1), :], tile)
                gain[c, i, half] = tile


def unrolled(count):
    def run(act):
        for i in range(count):
            act(i)

    return run


def scan_transform(h, r, rp, cst, f, store, wy, wx, perm):
    def loop(count):
        return unrolled(count) if h == 0 else pl.loop(0, count)

    @loop(4)
    def _(j):
        parts = [r[h, pl.ds((4 * j + t) * 16, 16)].astype(F32).reshape(128, 128) for t in range(4)]
        moved = dot(jnp.concatenate(parts, axis=1).astype(BF16), perm[...]).astype(BF16)
        for s in range(4):
            rp[s, j] = moved[:, s * 128 : (s + 1) * 128]

    @loop(2)
    def _(k2):
        lhs = jnp.concatenate(
            [jnp.concatenate([rp[2 * k2 + x2, j] for j in range(4)], axis=1) for x2 in range(2)], axis=0
        )
        for c in range(2):
            cst[c * 256 : (c + 1) * 256, :] = dot(lhs, wy[:, c * 512 : (c + 1) * 512]).astype(BF16)
        for c in range(2):
            res = dot(wx[c], cst[...]).astype(BF16)
            for t in range(4):
                f[t, 2 * c + k2] = res[:, t * 128 : (t + 1) * 128]

    @loop(4)
    def _(t):
        lhs = jnp.concatenate([f[t, s] for s in range(4)], axis=1)
        res = dot(lhs, perm[...])
        for q in range(4):
            store(4 * t + q, res[:, q * 128 : (q + 1) * 128])


def gather_pixels(z, count, half, raw, low, swap, unroll):
    def gather(v):
        first = v + 8 * half if count == 16 else v
        halves = [z[pl.ds(dh * 128 * count + first, 128, stride=count), :].T for dh in range(2)]
        turned = jnp.concatenate(halves, axis=1).astype(BF16)
        rows = jnp.concatenate([turned[s * 32 : (s + 1) * 32, :] for s in range(4)], axis=1)
        raw[pl.ds(v * 32 if unroll else pl.multiple_of(v * 32, 32), 32), :] = rows

    if unroll:
        for v in range(8):
            gather(v)
    else:
        pl.loop(0, 8)(gather)
    low[half * 256 : (half + 1) * 256, :] = dot(swap[...], raw[...]).astype(BF16)


def exchange_kernel(
    frames, probe, wy_h, wx_h, perm_h, swap_h, det_h, spec, gain,
    x, pv, prb, wy, wx, perm, swap, det, xs, z, m1, r, rp, cst, f, m2, m3, r2, r3, raw, low, ddr, ddi, pf, chi, sre, sim,
    load_sem, prb_send, prb_recv, send, recv,
):
    g, m = lax.axis_index("grp"), lax.axis_index("mem")
    me = g * 16 + m

    px, core, py = g // 4, lax.rem(g, 2), lax.rem(m, 4)
    pz = lax.rem(g // 2, 2) * 4 + m // 4
    turns = []
    for dz in (4, 3, 5, 2, 6, 1, 7, 0):
        z1 = lax.rem(pz + dz, 8)
        turns.append(((z1 // 4) * 2, lax.rem(z1, 4) * 4))

    def to_all(act):
        @pl.loop(1, 32)
        def _(i):
            step = 32 - i
            a = lax.rem(px + lax.rem(step // 2, 4), 4) * 4 + lax.rem(core + lax.rem(step, 2), 2)
            b = lax.rem(py + step // 8, 4)
            for za, zb in turns:
                act(a + za, b + zb)

        for za, zb in turns[:-1]:
            act(px * 4 + core + za, py + zb)

    def push(n, src, dst, a, b):
        pltpu.make_async_remote_copy(
            src_ref=src, dst_ref=dst, send_sem=send.at[n], recv_sem=recv.at[n], device_id=(a, b), device_id_type=MESH
        ).start()

    def arrived(n, ref):
        pltpu.make_async_copy(ref, ref, recv.at[n]).wait()

    loads = [
        pltpu.make_async_copy(src, dst, load_sem.at[n])
        for n, (src, dst) in enumerate(
            ((frames, x), (probe, pv), (wy_h, wy), (wx_h, wx), (perm_h, perm), (swap_h, swap), (det_h, det))
        )
    ]
    for load in loads:
        load.start()
    barrier = pltpu.get_barrier_semaphore()
    to_all(lambda a, b: pl.semaphore_signal(barrier, inc=1, device_id=(a, b), device_id_type=MESH))

    loads[0].wait()
    loads[1].wait()
    arrange_frames(0, x, xs, z, m1)
    pl.semaphore_wait(barrier, 255)

    for h in range(2):
        if h == 1:
            arrange_frames(1, x, xs, z, m1)
        pltpu.make_async_copy(m1.at[h, me], r.at[h, me], recv.at[h]).start()
        to_all(lambda a, b: push(h, m1.at[h, a * 16 + b], r.at[h, me], a, b))
        if h == 0:
            pltpu.make_async_copy(pv, prb.at[m], prb_recv).start()

            @pl.loop(1, 16)
            def _(i):
                pltpu.make_async_remote_copy(
                    src_ref=pv, dst_ref=prb.at[m], send_sem=prb_send, recv_sem=prb_recv,
                    device_id=(g, lax.rem(m + i, 16)), device_id_type=MESH,
                ).start()

    for load in loads[2:]:
        load.wait()

    arrived(0, r.at[0])

    def store_first(b, tile):
        m2[b] = tile.astype(BF16)

    scan_transform(0, r, rp, cst, f, store_first, wy, wx, perm)
    here = pl.ds(pl.multiple_of(me * 16, 16), 16)
    pltpu.make_async_copy(m2.at[m, pl.ds(pl.multiple_of(g * 16, 16), 16)], r2.at[here], recv.at[2]).start()
    to_all(lambda a, b: push(2, m2.at[b, pl.ds(pl.multiple_of(a * 16, 16), 16)], r2.at[here], a, b))

    arrived(1, r.at[1])

    def store_second(b, tile):
        m3[b] = tile.reshape(32, 8, 128).astype(BF16)

    scan_transform(1, r, rp, cst, f, store_second, wy, wx, perm)
    for half in range(2):
        pltpu.make_async_copy(m3.at[m, 2 * g + half], r3.at[half, me], recv.at[3 + half]).start()
        to_all(lambda a, b: push(3 + half, m3.at[b, 2 * a + half], r3.at[half, me], a, b))

    detector_table(det, ddr, ddi)
    pltpu.make_async_copy(prb, prb, prb_recv).wait()
    probe_products(g, m, prb, pf)
    wiener_gain(pf, ddr, ddi, chi, gain)

    arrived(2, r2)
    z[...] = r2[...].astype(F32)
    for half in range(2):
        gather_pixels(z, 16, half, raw, low, swap, False)

    @pl.loop(0, 4)
    def _(n):
        lanes = pl.ds(pl.multiple_of(n * 256, 256), 256)
        sre[n] = dot(low[...], ddr[0, :, lanes])
        sim[n] = dot(low[...], ddi[0, :, lanes])

    for half in range(2):
        arrived(3 + half, r3.at[half])
        z[0:2048, :] = r3[half].astype(F32).reshape(2048, 128)
        gather_pixels(z, 8, half, raw, low, swap, half == 1)
        rows = slice(half * 256, (half + 1) * 256)

        for n in range(4):
            lanes = slice(n * 256, (n + 1) * 256)
            spec[0, rows, lanes] = (sre[n, rows, :] + dot(low[rows, :], ddr[1, :, lanes])).astype(BF16)
            spec[1, rows, lanes] = (sim[n, rows, :] + dot(low[rows, :], ddi[1, :, lanes])).astype(BF16)


    pltpu.make_async_copy(prb.at[pl.ds(0, 15)], prb.at[pl.ds(0, 15)], prb_send).wait()
    for n, ref in enumerate((r.at[0], r.at[1], None, r3.at[0], r3.at[1])):
        ref = r2.at[pl.ds(0, 255 * 16)] if ref is None else ref.at[pl.ds(0, 255)]
        pltpu.make_async_copy(ref, ref, send.at[n]).wait()


def exchange(frames, probe):
    wy, wx, perm, swap, det = (jnp.asarray(t) for t in tables())
    hbm = pl.BlockSpec(memory_space=pl.ANY)
    vmem = pl.BlockSpec(memory_space=pltpu.VMEM)
    dma = pltpu.SemaphoreType.DMA
    return pl.pallas_call(
        exchange_kernel,
        out_shape=(pltpu.VMEM((2, 512, 1024), BF16), pltpu.VMEM((2, 8, 2, 8, 1024), F32)),
        in_specs=[hbm] * 7,
        out_specs=(vmem, vmem),
        scratch_shapes=[
            pltpu.VMEM((512, 1024), BF16),
            pltpu.VMEM((2, 8, 128), F32),
            pltpu.VMEM((16, 2, 8, 128), F32),
            pltpu.VMEM((512, 1024), BF16),
            pltpu.VMEM((2, 256, 512), BF16),
            pltpu.VMEM((512, 512), BF16),
            pltpu.VMEM((256, 256), BF16),
            pltpu.VMEM((4, 32, 1024), F32),
            pltpu.VMEM((4, 512, 128), F32),
            pltpu.VMEM((4096, 128), F32),
            pltpu.VMEM((2, 256, 8, 128), BF16),
            pltpu.VMEM((2, 256, 8, 128), BF16),
            pltpu.VMEM((4, 4, 128, 128), BF16),
            pltpu.VMEM((512, 512), BF16),
            pltpu.VMEM((4, 4, 256, 128), BF16),
            pltpu.VMEM((16, 256, 128), BF16),
            pltpu.VMEM((16, 32, 8, 128), BF16),
            pltpu.VMEM((4096, 128), BF16),
            pltpu.VMEM((2, 256, 8, 128), BF16),
            pltpu.VMEM((256, 1024), BF16),
            pltpu.VMEM((512, 1024), BF16),
            pltpu.VMEM((2, 1024, 1024), BF16),
            pltpu.VMEM((2, 1024, 1024), BF16),
            pltpu.VMEM((2, 64, 1024), F32),
            pltpu.VMEM((2, 64, 1024), F32),
            pltpu.VMEM((4, 512, 256), F32),
            pltpu.VMEM((4, 512, 256), F32),
            dma((7,)), dma, dma, dma((5,)), dma((5,)),
        ],
        compiler_params=pltpu.CompilerParams(collective_id=0, has_side_effects=True, vmem_limit_bytes=52 << 20),
    )(frames, probe, wy, wx, perm, swap, det)


def quotient_kernel(spec, gain, out_re, out_im):
    n = pl.program_id(0)
    for half in range(2):
        g_re, g_im = gain[0, n, half], gain[1, n, half]
        rows = pl.ds(pl.multiple_of(half * 256 + n * 32, 32), 32)
        s_re, s_im = spec[0, rows, :].astype(F32), spec[1, rows, :].astype(F32)
        for u in range(4):
            a, b = s_re[u * 8 : u * 8 + 8, :], s_im[u * 8 : u * 8 + 8, :]
            out_re[u, half * 8 : half * 8 + 8, :] = a * g_re + b * g_im
            out_im[u, half * 8 : half * 8 + 8, :] = b * g_re - a * g_im


def quotient(spec, gain):
    vmem = pl.BlockSpec(memory_space=pltpu.VMEM)
    return pl.pallas_call(
        quotient_kernel,
        grid=(8,),
        out_shape=(jax.ShapeDtypeStruct((32, 16, 1024), F32),) * 2,
        in_specs=[vmem, vmem],
        out_specs=(pl.BlockSpec((4, 16, 1024), lambda n: (n, 0, 0)),) * 2,
        compiler_params=pltpu.CompilerParams(vmem_limit_bytes=16 << 20),
    )(spec, gain)


def shards(frames, probe_wave):
    spec, gain = exchange(frames.reshape(512, PIX), probe_wave)
    return quotient(spec, gain)


def solution(mesh):
    return jax.shard_map(
        shards,
        mesh=mesh,
        in_specs=(P("grp", "mem", None), P(None, "mem", None)),
        out_specs=(P("mem", "grp", None), P("mem", "grp", None)),
        check_vma=False,
    )
```
